32 devices in a mesh: groups: 2 (over y), row: 4 (over z), col: 4 (over x, core).
Axes of the slice: x: 2, y: 2, z: 4, core: 2. Of those that a mesh axis runs over, the one named last changes fastest.
Arguments:
- seq_feat: bfloat16 [64, 256], P(('groups', 'row', 'col')), parts along dimension 0, may hold values from -6 to 6
- lengths: int32 [4], P('groups'), parts along dimension 0, may hold values from 1 to 24, 32 in all
- embed_weight: bfloat16 [2, 256, 128], replicated, may hold values from -0.375 to 0.375
- norm_gain: float32 [4, 128], replicated, may hold values from 0.1 to 1.9
- conv_weight: bfloat16 [4, 3, 3, 128, 128], replicated, may hold values from -0.1875 to 0.1875
- proj_weight: bfloat16 [4, 128, 128], replicated, may hold values from -0.5 to 0.5
- pair_cotangent: bfloat16 [64, 32, 128], P(('groups', 'row'), 'col'), parts along dimension 0, may hold values from -13 to 13
Outputs:
- pair_output: bfloat16 [64, 32, 128], P(('groups', 'row'), 'col'), parts along dimension 0
- seq_grad: float32 [64, 256], P(('groups', 'row', 'col')), parts along dimension 0
- embed_grad: float32 [4, 256, 128], P('groups'), parts along dimension 0
- gain_grad: float32 [8, 128], P('groups'), parts along dimension 0
- conv_grad: float32 [8, 3, 3, 128, 128], P('groups'), parts along dimension 0
- proj_grad: float32 [8, 128, 128], P('groups'), parts along dimension 0
The draws below stay inside these ranges and needn't reach their ends.
There are 2 independent parts, one for each index of `groups`. The reference program is written for one: setup_inputs(seed, part) draws one part's arguments, and reference() takes and returns one part's arrays. A program takes and returns all parts, laid end to end along the dimension named above; an argument that names none is the same for every part. Nothing has to cross between parts.
Inputs may be any that keep to these rules, and one draw needn't show every extreme that they name: lengths[0] residues are real; those at and after index lengths[0] are padding; the two entries sum to 32.
All inputs are finite; a program needn't handle non-finite values.
Results may differ from the reference program's by a relative error of at most 0.014.
Values may be sent and summed in bfloat16 or wider, within the bound.
No kernel may reach another device: no remote copies, remote signals or barrier semaphores. Data moves between devices by JAX's collectives and lax.ppermute only.
A program may use at most 64 MiB of HBM per device.

```python
import math
import jax
import jax.numpy as jnp
import numpy as np
from jax import lax

CH = 128
SEQ = 256
LAYERS = 4
L = 32


def draw_pair_cotangent(key, part):
    noise_key, row_key, col_key = jax.random.split(jax.random.fold_in(key, 11), 3)
    noise_field = jnp.clip(jax.random.normal(noise_key, (L, L, CH), jnp.float32), -4.0, 4.0)
    row_scale = jnp.exp(jax.random.uniform(row_key, (L,), jnp.float32, -0.575, 0.575))
    col_scale = jnp.exp(jax.random.uniform(col_key, (L,), jnp.float32, -0.575, 0.575))
    return (noise_field * row_scale[:, None, None] * col_scale[None, :, None]).astype(jnp.bfloat16)


def shard_levels(key, shape, cuts, smallest, largest):
    def one(dim, shards_of):
        heights = jax.random.uniform(jax.random.fold_in(jax.random.fold_in(key, 6), dim), (shards_of,), jnp.float32, smallest / len(cuts), largest / len(cuts))
        return jnp.repeat(jnp.exp(heights), shape[dim] // shards_of).reshape((-1,) + (1,) * (len(shape) - dim - 1))

    level = one(*cuts[0])
    for cut in cuts[1:]:
        level = level * one(*cut)
    return level


def length_profile(number_of, total, bound, slope):
    weights = [(1 << 20) // math.isqrt(rank ** slope) + 1 for rank in range(2, number_of + 1)]
    surplus, given = total - bound - (number_of - 1), [1] * (number_of - 1)
    while surplus > 0:
        free = [i for i in range(number_of - 1) if given[i] < bound]
        pool, left = sum([weights[i] for i in free]), surplus
        for i in free:
            addition = min(bound - given[i], max(1, left * weights[i] // pool), surplus)
            given[i] = given[i] + addition
            surplus = surplus - addition
    return np.array([bound] + given)


def uneven_parts(key, amount, total, most, slope):
    if amount == 2:
        one = jax.random.randint(key, (), max(1, total - most), min(most, total - 1) + 1)
        return jnp.stack([one, total - one])
    sizes = jnp.asarray(length_profile(amount, total, most, slope), jnp.int32)
    twos = (amount - 1) // 2
    donor, taker = sizes[1:1 + 2 * twos:2], sizes[2:2 + 2 * twos:2]
    margin = jnp.minimum(donor - 1, most - taker)
    shifted = jax.random.randint(jax.random.fold_in(key, 1), (twos,), 0, 1 << 20) % (margin + 1)
    sizes = sizes.at[1:1 + 2 * twos:2].set(donor - shifted).at[2:2 + 2 * twos:2].set(taker + shifted)
    return sizes[jax.random.permutation(jax.random.fold_in(key, 2), amount)]


def noise(stream_key, shape, deviation, limit, cuts=(), kind=jnp.bfloat16):
    result = jax.random.normal(stream_key, shape, jnp.float32) * deviation
    if len(cuts) > 0:
        result = shard_levels(stream_key, shape, cuts, -0.22, 0.18) * result
    return jnp.clip(result, min=-limit, max=limit).astype(kind)


def setup_inputs(seed: int = 0, part: int = 0) -> dict:
    seeds = jax.random.split(jax.random.key(seed), 8)
    part_keys = jax.random.split(jax.random.fold_in(seeds[7], part), 8)
    seq_feat = noise(part_keys[0], (L, SEQ), 1.0, 6.0, ((0, 16),))
    lengths = uneven_parts(part_keys[1], 2, L, L - L // 4, 0).astype(jnp.int32)
    embed_weight = noise(seeds[2], (2, SEQ, CH), SEQ ** -0.5, 0.375)
    norm_gain = jnp.clip(1.0 + 0.18 * jax.random.normal(seeds[3], (LAYERS, CH), jnp.float32), 0.1, 1.9)
    conv_weight = noise(seeds[4], (LAYERS, 3, 3, CH, CH), (9 * CH) ** -0.5, 0.1875)
    proj_weight = noise(seeds[5], (LAYERS, CH, CH), CH ** -0.5, 0.5)
    pair_cotangent = draw_pair_cotangent(jax.random.fold_in(jax.random.fold_in(seeds[7], part), 71), part)
    return {"seq_feat": seq_feat, "lengths": lengths, "embed_weight": embed_weight, "norm_gain": norm_gain, "conv_weight": conv_weight, "proj_weight": proj_weight, "pair_cotangent": pair_cotangent}


eps = 1e-05

def elu_slope(values):
    return jnp.where(values > 0, 1.0, jnp.exp(jnp.minimum(values, 0.0)))

def normalize(stream, gain_row):
    average = lax.optimization_barrier(jnp.mean(stream, axis=-1, keepdims=True))
    centred = stream - average
    variance = lax.optimization_barrier(jnp.mean(centred * centred, axis=-1, keepdims=True))
    inv_std = lax.rsqrt(variance + eps)
    normalized = centred * inv_std
    return (normalized, inv_std, normalized * gain_row)

def conv_forward(padded, weight, spacing, height, width):
    channels = padded.shape[-1]
    summed = jnp.zeros((height * width, weight.shape[-1]), jnp.float32)
    for tap_row in range(3):
        for tap_col in range(3):
            window = padded[tap_row * spacing:tap_row * spacing + height, tap_col * spacing:tap_col * spacing + width, :]
            summed = summed + jnp.dot(window.reshape(height * width, channels), weight[tap_row, tap_col], preferred_element_type=jnp.float32)
    return summed.reshape(height, width, -1)

def conv_backward(padded, weight, spacing, height, width):
    channels = padded.shape[-1]
    summed = jnp.zeros((height * width, weight.shape[-2]), jnp.float32)
    for tap_row in range(3):
        for tap_col in range(3):
            start_row = (2 - tap_row) * spacing
            start_col = (2 - tap_col) * spacing
            window = padded[start_row:start_row + height, start_col:start_col + width, :]
            summed = summed + jnp.dot(window.reshape(height * width, channels), weight[tap_row, tap_col].T, preferred_element_type=jnp.float32)
    return summed.reshape(height, width, -1)

def conv_weight_grad(padded, grad_tile, spacing, height, width):
    channels = padded.shape[-1]
    flat_grad = grad_tile.reshape(height * width, -1)
    terms = []
    for tap_row in range(3):
        row_terms = []
        for tap_col in range(3):
            window = padded[tap_row * spacing:tap_row * spacing + height, tap_col * spacing:tap_col * spacing + width, :]
            row_terms.append(lax.dot_general(window.reshape(height * width, channels), flat_grad, (((0,), (0,)), ((), ())), preferred_element_type=jnp.float32))
        terms.append(jnp.stack(row_terms))
    return jnp.stack(terms)

def reference(seq_feat, lengths, embed_weight, norm_gain, conv_weight, proj_weight, pair_cotangent):
    residues = seq_feat.shape[0]
    channels = embed_weight.shape[-1]
    live_rows = (jnp.arange(residues, dtype=jnp.int32) < lengths[0]).astype(jnp.float32)
    live_mask = live_rows[:, None, None] * live_rows[None, :, None]
    row_emb = jnp.dot(seq_feat, embed_weight[0], preferred_element_type=jnp.float32).astype(jnp.bfloat16)
    col_emb = jnp.dot(seq_feat, embed_weight[1], preferred_element_type=jnp.float32).astype(jnp.bfloat16)
    stream = live_mask * (row_emb.astype(jnp.float32)[:, None, :] + col_emb.astype(jnp.float32)[None, :, :])
    stored = []
    for layer_number in range(LAYERS):
        spacing = 2 ** layer_number
        normalized, inv_std, scaled = normalize(stream, norm_gain[layer_number])
        squashed = (live_mask * jax.nn.elu(scaled)).astype(jnp.bfloat16)
        padded = jnp.pad(squashed, ((spacing, spacing), (spacing, spacing), (0, 0)))
        convolved = conv_forward(padded, conv_weight[layer_number], spacing, residues, residues)
        excited = jax.nn.elu(convolved).astype(jnp.bfloat16)
        update = jnp.dot(excited.reshape(-1, channels), proj_weight[layer_number], preferred_element_type=jnp.float32).reshape(residues, residues, channels)
        stored.append((stream, padded, convolved, excited))
        stream = stream + live_mask * update
    pair_output = stream.astype(jnp.bfloat16)
    grad_scale = 1.0 / residues
    back_grad = pair_cotangent.astype(jnp.float32)
    gain_terms = [None] * LAYERS
    conv_terms = [None] * LAYERS
    proj_terms = [None] * LAYERS
    for layer_number in reversed(range(LAYERS)):
        spacing = 2 ** layer_number
        old_stream, padded, convolved, excited = stored[layer_number]
        masked = (live_mask * back_grad).astype(jnp.bfloat16)
        flat_masked = masked.reshape(-1, channels)
        proj_terms[layer_number] = lax.dot_general(excited.reshape(-1, channels), flat_masked, (((0,), (0,)), ((), ())), preferred_element_type=jnp.float32) * grad_scale
        d_excited = jnp.dot(flat_masked, proj_weight[layer_number].T, preferred_element_type=jnp.float32).reshape(residues, residues, channels)
        d_pre = (d_excited * elu_slope(convolved)).astype(jnp.bfloat16)
        conv_terms[layer_number] = conv_weight_grad(padded, d_pre, spacing, residues, residues) * grad_scale
        d_padded = jnp.pad(d_pre, ((spacing, spacing), (spacing, spacing), (0, 0)))
        d_squashed = conv_backward(d_padded, conv_weight[layer_number], spacing, residues, residues)
        normalized, inv_std, scaled = normalize(old_stream, norm_gain[layer_number])
        d_scaled = live_mask * d_squashed * elu_slope(scaled)
        gain_terms[layer_number] = lax.optimization_barrier(jnp.sum(d_scaled * normalized, axis=(0, 1))) * grad_scale
        d_norm = d_scaled * norm_gain[layer_number]
        back_grad = back_grad + inv_std * (d_norm - lax.optimization_barrier(jnp.mean(d_norm, axis=-1, keepdims=True)) - normalized * lax.optimization_barrier(jnp.mean(d_norm * normalized, axis=-1, keepdims=True)))
    final_masked = live_mask * back_grad
    d_row = lax.optimization_barrier(jnp.sum(final_masked, axis=1)).astype(jnp.bfloat16)
    d_col = lax.optimization_barrier(jnp.sum(final_masked, axis=0)).astype(jnp.bfloat16)
    seq_grad = (jnp.dot(d_row, embed_weight[0].T, preferred_element_type=jnp.float32) + jnp.dot(d_col, embed_weight[1].T, preferred_element_type=jnp.float32)) / math.sqrt(residues)
    embed_grad = jnp.stack([lax.dot_general(seq_feat, d_row, (((0,), (0,)), ((), ())), preferred_element_type=jnp.float32), lax.dot_general(seq_feat, d_col, (((0,), (0,)), ((), ())), preferred_element_type=jnp.float32)]) * grad_scale
    return (pair_output, seq_grad, embed_grad, jnp.stack(gain_terms), jnp.stack(conv_terms), jnp.stack(proj_terms))
```

```python
import functools
import math

import jax
import jax.numpy as jnp
from jax import lax
from jax.experimental import pallas as pl
from jax.experimental.pallas import tpu as pltpu
from jax.sharding import PartitionSpec as P

LAYERS = 4


eps = 1e-05


def with_halo(x, sides, width):
    for axis, dim in sides:
        count, length = (lax.axis_size(axis), x.shape[dim])
        up = [(i, (i + 1) % count) for i in range(count - 1)]
        down = [(j, i) for i, j in up]
        last = lax.slice_in_dim(x, length - width, length, axis=dim)
        first = lax.slice_in_dim(x, 0, width, axis=dim)
        before = lax.ppermute(last, axis, up)
        after = lax.ppermute(first, axis, down)
        x = jnp.concatenate([before, x, after], axis=dim)
    return x


def elu_slope(values):
    return jnp.where(values > 0, 1.0, jnp.exp(jnp.minimum(values, 0.0)))


def normalize(stream, gain_row):
    average = jnp.mean(stream, axis=-1, keepdims=True)
    centred = stream - average
    variance = jnp.mean(centred * centred, axis=-1, keepdims=True)
    inv_std = lax.rsqrt(variance + eps)
    normalized = centred * inv_std
    return (normalized, inv_std, normalized * gain_row)


def conv_forward(padded, weight, spacing, height, width):
    channels = padded.shape[-1]
    summed = jnp.zeros((height * width, weight.shape[-1]), jnp.float32)
    for tap_row in range(3):
        for tap_col in range(3):
            window = padded[
                tap_row * spacing : tap_row * spacing + height,
                tap_col * spacing : tap_col * spacing + width,
                :,
            ]
            summed = summed + jnp.dot(
                window.reshape(height * width, channels),
                weight[tap_row, tap_col],
                preferred_element_type=jnp.float32,
            )
    return summed.reshape(height, width, -1)


def conv_backward(padded, weight, spacing, height, width):
    channels = padded.shape[-1]
    summed = jnp.zeros((height * width, weight.shape[-2]), jnp.float32)
    for tap_row in range(3):
        for tap_col in range(3):
            start_row = (2 - tap_row) * spacing
            start_col = (2 - tap_col) * spacing
            window = padded[start_row : start_row + height, start_col : start_col + width, :]
            summed = summed + jnp.dot(
                window.reshape(height * width, channels),
                weight[tap_row, tap_col].T,
                preferred_element_type=jnp.float32,
            )
    return summed.reshape(height, width, -1)


def conv_weight_grad(padded, grad_tile, spacing, height, width):
    channels = padded.shape[-1]
    flat_grad = grad_tile.reshape(height * width, -1)
    terms = []
    for tap_row in range(3):
        row_terms = []
        for tap_col in range(3):
            window = padded[
                tap_row * spacing : tap_row * spacing + height,
                tap_col * spacing : tap_col * spacing + width,
                :,
            ]
            row_terms.append(
                lax.dot_general(
                    window.reshape(height * width, channels),
                    flat_grad,
                    (((0,), (0,)), ((), ())),
                    preferred_element_type=jnp.float32,
                )
            )
        terms.append(jnp.stack(row_terms))
    return jnp.stack(terms)


def tiled_body(seq_feat, lengths, embed_weight, norm_gain, conv_weight, proj_weight, pair_cotangent):
    tile_rows = pair_cotangent.shape[0]
    tile_cols = pair_cotangent.shape[1]
    channels = pair_cotangent.shape[2]
    residues = tile_rows * lax.axis_size("row")
    row_start = lax.axis_index("row") * tile_rows
    col_start = lax.axis_index("col") * tile_cols
    row_live = (row_start + jnp.arange(tile_rows, dtype=jnp.int32) < lengths[0]).astype(jnp.float32)
    col_live = (col_start + jnp.arange(tile_cols, dtype=jnp.int32) < lengths[0]).astype(jnp.float32)
    live_mask = row_live[:, None, None] * col_live[None, :, None]
    gathered = lax.all_gather(seq_feat, ("row", "col"), axis=0, tiled=True)
    row_part = lax.dynamic_slice_in_dim(gathered, row_start, tile_rows, 0)
    col_part = lax.dynamic_slice_in_dim(gathered, col_start, tile_cols, 0)
    row_emb = jnp.dot(row_part, embed_weight[0], preferred_element_type=jnp.float32).astype(
        jnp.bfloat16
    )
    col_emb = jnp.dot(col_part, embed_weight[1], preferred_element_type=jnp.float32).astype(
        jnp.bfloat16
    )
    stream = live_mask * (
        row_emb.astype(jnp.float32)[:, None, :] + col_emb.astype(jnp.float32)[None, :, :]
    )
    stored = []
    for layer_number in range(LAYERS):
        spacing = 2**layer_number
        normalized, inv_std, scaled = normalize(stream, norm_gain[layer_number])
        squashed = (live_mask * jax.nn.elu(scaled)).astype(jnp.bfloat16)
        padded = with_halo(squashed, (("row", 0), ("col", 1)), spacing)
        convolved = conv_forward(padded, conv_weight[layer_number], spacing, tile_rows, tile_cols)
        excited = jax.nn.elu(convolved).astype(jnp.bfloat16)
        update = jnp.dot(
            excited.reshape(-1, channels),
            proj_weight[layer_number],
            preferred_element_type=jnp.float32,
        ).reshape(tile_rows, tile_cols, channels)
        stored.append((stream, padded, convolved, excited))
        stream = stream + live_mask * update
    pair_output = stream.astype(jnp.bfloat16)
    grad_scale = 1.0 / residues
    back_grad = pair_cotangent.astype(jnp.float32)
    gain_terms = [None] * LAYERS
    conv_terms = [None] * LAYERS
    proj_terms = [None] * LAYERS
    for layer_number in reversed(range(LAYERS)):
        spacing = 2**layer_number
        old_stream, padded, convolved, excited = stored[layer_number]
        masked = (live_mask * back_grad).astype(jnp.bfloat16)
        flat_masked = masked.reshape(-1, channels)
        proj_term = (
            lax.dot_general(
                excited.reshape(-1, channels),
                flat_masked,
                (((0,), (0,)), ((), ())),
                preferred_element_type=jnp.float32,
            )
            * grad_scale
        )
        d_excited = jnp.dot(
            flat_masked, proj_weight[layer_number].T, preferred_element_type=jnp.float32
        ).reshape(tile_rows, tile_cols, channels)
        d_pre = (d_excited * elu_slope(convolved)).astype(jnp.bfloat16)
        conv_term = conv_weight_grad(padded, d_pre, spacing, tile_rows, tile_cols) * grad_scale
        d_padded = with_halo(d_pre, (("row", 0), ("col", 1)), spacing)
        d_squashed = conv_backward(
            d_padded, conv_weight[layer_number], spacing, tile_rows, tile_cols
        )
        normalized, inv_std, scaled = normalize(old_stream, norm_gain[layer_number])
        d_scaled = live_mask * d_squashed * elu_slope(scaled)
        gain_term = jnp.sum(d_scaled * normalized, axis=(0, 1)) * grad_scale
        d_norm = d_scaled * norm_gain[layer_number]
        back_grad = back_grad + inv_std * (
            d_norm
            - jnp.mean(d_norm, axis=-1, keepdims=True)
            - normalized * jnp.mean(d_norm * normalized, axis=-1, keepdims=True)
        )
        gain_terms[layer_number] = gain_term
        conv_terms[layer_number] = conv_term
        proj_terms[layer_number] = proj_term
    final_masked = live_mask * back_grad
    row_totals = jnp.sum(final_masked, axis=1)
    col_totals = jnp.sum(final_masked, axis=0)
    d_row = lax.psum_scatter(row_totals, "col", scatter_dimension=0, tiled=True).astype(
        jnp.bfloat16
    )
    spread_cols = lax.dynamic_update_slice_in_dim(
        jnp.zeros((residues, channels), jnp.float32), col_totals, col_start, 0
    )
    d_col = lax.psum_scatter(spread_cols, ("row", "col"), scatter_dimension=0, tiled=True).astype(
        jnp.bfloat16
    )
    seq_grad = (
        jnp.dot(d_row, embed_weight[0].T, preferred_element_type=jnp.float32)
        + jnp.dot(d_col, embed_weight[1].T, preferred_element_type=jnp.float32)
    ) / math.sqrt(residues)
    embed_term = (
        jnp.stack(
            [
                lax.dot_general(
                    seq_feat, d_row, (((0,), (0,)), ((), ())), preferred_element_type=jnp.float32
                ),
                lax.dot_general(
                    seq_feat, d_col, (((0,), (0,)), ((), ())), preferred_element_type=jnp.float32
                ),
            ]
        )
        * grad_scale
    )
    gain_grad = jnp.stack(gain_terms)
    conv_grad = jnp.stack(conv_terms)
    proj_grad = jnp.stack(proj_terms)
    gain_grad, conv_grad, proj_grad, embed_grad = lax.psum(
        (gain_grad, conv_grad, proj_grad, embed_term), ("row", "col")
    )
    return (pair_output, seq_grad, embed_grad, gain_grad, conv_grad, proj_grad)


NT = (((1,), (1,)), ((), ()))
TN = (((0,), (0,)), ((), ()))
NN = (((1,), (0,)), ((), ()))


def dot(a, b, dims):
    return lax.dot_general(a, b, dims, preferred_element_type=jnp.float32)


def most_live(residues):
    return residues - residues // 4


def block_kernel(
    grid_rows,
    grid_cols,
    lengths_ref,
    *refs,
):
    pieces, (embed_ref, gain_ref, conv_hbm, proj_ref) = refs[:4], refs[4:8]
    (pair_ref, seq_grad_ref, embed_grad_ref, gain_grad_ref, conv_grad_hbm, proj_grad_ref) = refs[8:14]
    (
        weights,
        weight_sem,
        stream,
        back,
        live,
        shifted,
        taps,
        normed,
        inv,
        slope,
        squashed,
        conv_slope,
        excited,
        masked,
        spread,
        seq_lo,
        seq_hi,
        conv_grad,
        grad_sem,
    ) = refs[14:]
    tile_rows, tile_cols, channels = pair_ref.shape
    residues = tile_rows * grid_rows
    own = seq_grad_ref.shape[0]
    height = most_live(residues)
    pitch = residues
    count = height * pitch
    margin = 2 ** (LAYERS - 1)
    pad = margin * pitch
    chunk_rows = 8
    chunk = chunk_rows * pitch
    chunks = [slice(k * chunk, (k + 1) * chunk) for k in range(height // chunk_rows)]
    row, col = lax.axis_index("row"), lax.axis_index("col")
    live_count = lengths_ref[0]

    loads = [
        pltpu.make_async_copy(conv_hbm.at[k], weights.at[k], weight_sem.at[k])
        for k in range(LAYERS)
    ]
    for load in loads:
        load.start()

    piece_rows = pieces[0].shape[0] // grid_rows
    tile = tile_rows * tile_cols
    half = seq_lo.shape[1]
    for step_col in range(grid_cols):
        source_col = lax.rem(col + grid_cols - step_col, grid_cols)
        for step_row in range(grid_rows):
            source_row = lax.rem(row + grid_rows - step_row, grid_rows)
            piece = pieces[step_col][step_row * piece_rows : (step_row + 1) * piece_rows, :].astype(
                jnp.float32
            )
            back[
                pl.ds(pl.multiple_of(source_row * tile_rows, tile_rows), tile_rows),
                pl.ds(pl.multiple_of(source_col * tile_cols, tile_cols), tile_cols),
                :,
            ] = piece[:tile].reshape(tile_rows, tile_cols, channels)
            owner = source_row * grid_cols + source_col
            spread[pl.ds(pl.multiple_of(owner * 8, 8), 8), :] = piece[tile : tile + 8]
    owners = grid_rows * grid_cols
    for k in range(own):
        seq_lo[pl.ds(k, owners, stride=own), :] = spread[pl.ds(k, owners, stride=8), :]
        seq_hi[pl.ds(k, owners, stride=own), :] = spread[pl.ds(own + k, owners, stride=8), :]
    seq = jnp.concatenate([seq_lo[...], seq_hi[...]], axis=1).astype(jnp.bfloat16)

    pixel = lax.broadcasted_iota(jnp.int32, (residues, pitch, channels), 0)
    pixel = jnp.maximum(pixel, lax.broadcasted_iota(jnp.int32, (residues, pitch, channels), 1))
    live[...] = (pixel < live_count).astype(jnp.float32)

    shifted[...] = jnp.zeros_like(shifted)
    taps[...] = jnp.zeros_like(taps)

    row_emb = dot(seq, embed_ref[0], NN).astype(jnp.bfloat16).astype(jnp.float32)
    col_emb = dot(seq, embed_ref[1], NN).astype(jnp.bfloat16).astype(jnp.float32)
    stream[...] = live[...] * (row_emb[:, None, :] + col_emb[None, :, :])

    flat = lambda ref: ref.reshape(residues * pitch, channels)
    stream_flat, live_flat, back_flat = flat(stream), flat(live), flat(back)

    def lane_mean(x):
        return jnp.mean(x, axis=-1, keepdims=True)

    def window(part, spacing, direction):
        return jnp.concatenate(
            [
                taps[
                    pad + part.start + direction * a * spacing * pitch : pad
                    + part.stop
                    + direction * a * spacing * pitch,
                    :,
                ]
                for a in (-1, 0, 1)
            ],
            axis=1,
        )

    def fill_taps(part, spacing, direction):
        for b in (-1, 0, 1):
            start = margin + part.start + direction * b * spacing
            taps[pad + part.start : pad + part.stop, (b + 1) * channels : (b + 2) * channels] = (
                shifted[start : start + chunk, :].astype(jnp.bfloat16)
            )

    for layer in range(LAYERS):
        spacing = 2**layer
        gain = gain_ref[layer : layer + 1, :]
        for part in chunks:
            value = stream_flat[part, :]
            centred = value - lane_mean(value)
            inv_std = lax.rsqrt(lane_mean(centred * centred) + eps)
            normalized = centred * inv_std
            scaled = normalized * gain
            decay = jnp.exp(jnp.minimum(scaled, 0.0))
            activated = jnp.maximum(scaled, 0.0) + (decay - 1.0)
            normed[layer, part, :] = normalized
            inv[layer, part, :] = jnp.broadcast_to(inv_std, normalized.shape)
            slope[layer, part, :] = decay * live_flat[part, :]
            shifted[margin + part.start : margin + part.stop, :] = activated
            squashed[layer, part, :] = activated.astype(jnp.bfloat16)
        for part in chunks:
            fill_taps(part, spacing, 1)
        loads[layer].wait()
        for part in chunks:
            convolved = dot(window(part, spacing, 1), weights[layer], NN)
            decay = jnp.exp(jnp.minimum(convolved, 0.0))
            conv_slope[layer, part, :] = decay
            hidden = (jnp.maximum(convolved, 0.0) + (decay - 1.0)).astype(jnp.bfloat16)
            excited[layer, part, :] = hidden
            update = dot(hidden, proj_ref[layer], NN)
            stream_flat[part, :] = stream_flat[part, :] + live_flat[part, :] * update

    pair_ref[...] = stream[
        pl.ds(pl.multiple_of(row * tile_rows, tile_rows), tile_rows),
        pl.ds(pl.multiple_of(col * tile_cols, tile_cols), tile_cols),
        :,
    ].astype(jnp.bfloat16)

    grad_scale = 1.0 / residues
    for part in chunks:
        back_flat[part, :] = back_flat[part, :] * live_flat[part, :]
    stores = []
    for layer in reversed(range(LAYERS)):
        spacing = 2**layer
        gain = gain_ref[layer : layer + 1, :]
        for part in chunks:
            grad = back_flat[part, :].astype(jnp.bfloat16)
            masked[part, :] = grad
            shifted[margin + part.start : margin + part.stop, :] = (
                dot(grad, proj_ref[layer], NT) * conv_slope[layer, part, :]
            )
        for part in chunks:
            fill_taps(part, spacing, -1)
        proj_grad_ref[layer] = dot(excited[layer], masked[...], TN) * grad_scale
        back_weights = jnp.concatenate(
            [weights[layer, t * channels : (t + 1) * channels, :] for t in range(9)], axis=1
        )
        gain_total = jnp.zeros((1, channels), jnp.float32)
        for part in chunks:
            d_squashed = dot(window(part, spacing, -1), back_weights, NT)
            normalized = normed[layer, part, :]
            d_scaled = d_squashed * slope[layer, part, :]
            gain_total = gain_total + jnp.sum(d_scaled * normalized, axis=0, keepdims=True)
            d_norm = d_scaled * gain
            back_flat[part, :] = back_flat[part, :] + inv[layer, part, :] * (
                d_norm - lane_mean(d_norm) - normalized * lane_mean(d_norm * normalized)
            )
        gain_grad_ref[layer : layer + 1, :] = gain_total * grad_scale
        every = slice(0, count)
        weight_grad = dot(squashed[layer], window(every, spacing, -1), TN) * grad_scale
        for t in range(9):
            conv_grad[layer, t] = weight_grad[:, t * channels : (t + 1) * channels]
        store = pltpu.make_async_copy(
            conv_grad.at[layer], conv_grad_hbm.at[layer], grad_sem.at[layer]
        )
        store.start()
        stores.append(store)

    final = back[...]
    beyond = lax.broadcasted_iota(jnp.int32, (residues, pitch, channels), 0) < height
    final = jnp.where(beyond, final, 0.0)
    d_row = jnp.sum(final, axis=1).astype(jnp.bfloat16)
    d_col = jnp.sum(final, axis=0).astype(jnp.bfloat16)
    embed_grad_ref[0] = dot(seq, d_row, TN) * grad_scale
    embed_grad_ref[1] = dot(seq, d_col, TN) * grad_scale
    seq_grad = (dot(d_row, embed_ref[0], NT) + dot(d_col, embed_ref[1], NT)) / math.sqrt(residues)
    first = own * (row * grid_cols + col)
    for k in range(own):
        chosen = lax.broadcasted_iota(jnp.int32, seq_grad.shape, 0) == first + k
        seq_grad_ref[k : k + 1, :] = jnp.sum(
            jnp.where(chosen, seq_grad, 0.0), axis=0, keepdims=True
        )
    for store in stores:
        store.wait()


def replicated_body(
    seq_feat, lengths, embed_weight, norm_gain, conv_weight, proj_weight, pair_cotangent
):
    tile_rows, tile_cols, channels = pair_cotangent.shape
    grid_rows, grid_cols = lax.axis_size("row"), lax.axis_size("col")
    residues = tile_rows * grid_rows
    height, pitch = most_live(residues), residues
    margin = 2 ** (LAYERS - 1)
    own, features = seq_feat.shape
    halves = features // channels
    seq_rows = jnp.concatenate(
        [seq_feat[:, k * channels : (k + 1) * channels] for k in range(halves)], axis=0
    )
    payload = jnp.concatenate(
        [
            pair_cotangent.reshape(tile_rows * tile_cols, channels),
            seq_rows,
            jnp.zeros((16 - own * halves, channels), jnp.bfloat16),
        ],
        axis=0,
    )

    def rotate(x, axis, count, step):
        return lax.ppermute(x, axis, [(i, (i + step) % count) for i in range(count)])

    column = jnp.concatenate(
        [payload] + [rotate(payload, "row", grid_rows, k) for k in range(1, grid_rows)], axis=0
    )
    pieces = [column] + [rotate(column, "col", grid_cols, k) for k in range(1, grid_cols)]
    count = height * pitch
    taps_rows = count + 2 * margin * pitch
    f32, bf16 = jnp.float32, jnp.bfloat16
    vmem = pl.BlockSpec(memory_space=pltpu.VMEM)
    hbm = pl.BlockSpec(memory_space=pl.ANY)
    outs = pl.pallas_call(
        functools.partial(block_kernel, grid_rows, grid_cols),
        out_shape=(
            jax.ShapeDtypeStruct((tile_rows, tile_cols, channels), bf16),
            jax.ShapeDtypeStruct((own, features), f32),
            jax.ShapeDtypeStruct((2, features, channels), f32),
            jax.ShapeDtypeStruct((LAYERS, channels), f32),
            jax.ShapeDtypeStruct((LAYERS, 9, channels, channels), f32),
            jax.ShapeDtypeStruct((LAYERS, channels, channels), f32),
        ),
        in_specs=[pl.BlockSpec(memory_space=pltpu.SMEM)] + [vmem] * 6 + [hbm, vmem],
        out_specs=(vmem, vmem, vmem, vmem, hbm, vmem),
        scratch_shapes=[
            pltpu.VMEM((LAYERS, 9 * channels, channels), bf16),
            pltpu.SemaphoreType.DMA((LAYERS,)),
            pltpu.VMEM((residues, pitch, channels), f32),
            pltpu.VMEM((residues, pitch, channels), f32),
            pltpu.VMEM((residues, pitch, channels), f32),
            pltpu.VMEM((count + 2 * margin, channels), f32),
            pltpu.VMEM((taps_rows, 3 * channels), bf16),
            pltpu.VMEM((LAYERS, count, channels), f32),
            pltpu.VMEM((LAYERS, count, channels), f32),
            pltpu.VMEM((LAYERS, count, channels), f32),
            pltpu.VMEM((LAYERS, count, channels), bf16),
            pltpu.VMEM((LAYERS, count, channels), f32),
            pltpu.VMEM((LAYERS, count, channels), bf16),
            pltpu.VMEM((count, channels), bf16),
            pltpu.VMEM((8 * grid_rows * grid_cols, channels), f32),
            pltpu.VMEM((residues, channels), f32),
            pltpu.VMEM((residues, channels), f32),
            pltpu.VMEM((LAYERS, 9, channels, channels), f32),
            pltpu.SemaphoreType.DMA((LAYERS,)),
        ],
        compiler_params=pltpu.CompilerParams(vmem_limit_bytes=48 * 1024 * 1024),
    )(
        lengths,
        *pieces,
        embed_weight,
        norm_gain,
        conv_weight.reshape(LAYERS, 9 * channels, channels),
        proj_weight,
    )
    pair_output, seq_grad, embed_grad, gain_grad, conv_grad, proj_grad = outs
    return (
        pair_output,
        seq_grad,
        embed_grad,
        gain_grad,
        conv_grad.reshape(LAYERS, 3, 3, channels, channels),
        proj_grad,
    )


def body(seq_feat, lengths, embed_weight, norm_gain, conv_weight, proj_weight, pair_cotangent):
    residues = pair_cotangent.shape[0] * lax.axis_size("row")
    plan = replicated_body if residues <= 32 else tiled_body
    return plan(
        seq_feat, lengths, embed_weight, norm_gain, conv_weight, proj_weight, pair_cotangent
    )


def solution(mesh):
    placed = (
        P(("groups", "row", "col"), None),
        P("groups"),
        P(),
        P(),
        P(),
        P(),
        P(("groups", "row"), "col", None),
    )
    return jax.shard_map(
        body,
        mesh=mesh,
        in_specs=placed,
        out_specs=(
            P(("groups", "row"), "col", None),
            P(("groups", "row", "col"), None),
            P("groups", None, None),
            P("groups", None),
            P("groups", None, None, None, None),
            P("groups", None, None),
        ),
        check_vma=False,
    )
```

```python
import functools
import math

import jax
import jax.numpy as jnp
from jax import lax
from jax.experimental import pallas as pl
from jax.experimental.pallas import tpu as pltpu
from jax.sharding import PartitionSpec as P

LAYERS = 4


eps = 1e-05


def with_halo(x, sides, width):
    for axis, dim in sides:
        count, length = (lax.axis_size(axis), x.shape[dim])
        up = [(i, (i + 1) % count) for i in range(count - 1)]
        down = [(j, i) for i, j in up]
        last = lax.slice_in_dim(x, length - width, length, axis=dim)
        first = lax.slice_in_dim(x, 0, width, axis=dim)
        before = lax.ppermute(last, axis, up)
        after = lax.ppermute(first, axis, down)
        x = jnp.concatenate([before, x, after], axis=dim)
    return x


def elu_slope(values):
    return jnp.where(values > 0, 1.0, jnp.exp(jnp.minimum(values, 0.0)))


def normalize(stream, gain_row):
    average = jnp.mean(stream, axis=-1, keepdims=True)
    centred = stream - average
    variance = jnp.mean(centred * centred, axis=-1, keepdims=True)
    inv_std = lax.rsqrt(variance + eps)
    normalized = centred * inv_std
    return (normalized, inv_std, normalized * gain_row)


def conv_forward(padded, weight, spacing, height, width):
    channels = padded.shape[-1]
    summed = jnp.zeros((height * width, weight.shape[-1]), jnp.float32)
    for tap_row in range(3):
        for tap_col in range(3):
            window = padded[
                tap_row * spacing : tap_row * spacing + height,
                tap_col * spacing : tap_col * spacing + width,
                :,
            ]
            summed = summed + jnp.dot(
                window.reshape(height * width, channels),
                weight[tap_row, tap_col],
                preferred_element_type=jnp.float32,
            )
    return summed.reshape(height, width, -1)


def conv_backward(padded, weight, spacing, height, width):
    channels = padded.shape[-1]
    summed = jnp.zeros((height * width, weight.shape[-2]), jnp.float32)
    for tap_row in range(3):
        for tap_col in range(3):
            start_row = (2 - tap_row) * spacing
            start_col = (2 - tap_col) * spacing
            window = padded[start_row : start_row + height, start_col : start_col + width, :]
            summed = summed + jnp.dot(
                window.reshape(height * width, channels),
                weight[tap_row, tap_col].T,
                preferred_element_type=jnp.float32,
            )
    return summed.reshape(height, width, -1)


def conv_weight_grad(padded, grad_tile, spacing, height, width):
    channels = padded.shape[-1]
    flat_grad = grad_tile.reshape(height * width, -1)
    terms = []
    for tap_row in range(3):
        row_terms = []
        for tap_col in range(3):
            window = padded[
                tap_row * spacing : tap_row * spacing + height,
                tap_col * spacing : tap_col * spacing + width,
                :,
            ]
            row_terms.append(
                lax.dot_general(
                    window.reshape(height * width, channels),
                    flat_grad,
                    (((0,), (0,)), ((), ())),
                    preferred_element_type=jnp.float32,
                )
            )
        terms.append(jnp.stack(row_terms))
    return jnp.stack(terms)


def tiled_body(seq_feat, lengths, embed_weight, norm_gain, conv_weight, proj_weight, pair_cotangent):
    tile_rows = pair_cotangent.shape[0]
    tile_cols = pair_cotangent.shape[1]
    channels = pair_cotangent.shape[2]
    residues = tile_rows * lax.axis_size("row")
    row_start = lax.axis_index("row") * tile_rows
    col_start = lax.axis_index("col") * tile_cols
    row_live = (row_start + jnp.arange(tile_rows, dtype=jnp.int32) < lengths[0]).astype(jnp.float32)
    col_live = (col_start + jnp.arange(tile_cols, dtype=jnp.int32) < lengths[0]).astype(jnp.float32)
    live_mask = row_live[:, None, None] * col_live[None, :, None]
    gathered = lax.all_gather(seq_feat, ("row", "col"), axis=0, tiled=True)
    row_part = lax.dynamic_slice_in_dim(gathered, row_start, tile_rows, 0)
    col_part = lax.dynamic_slice_in_dim(gathered, col_start, tile_cols, 0)
    row_emb = jnp.dot(row_part, embed_weight[0], preferred_element_type=jnp.float32).astype(
        jnp.bfloat16
    )
    col_emb = jnp.dot(col_part, embed_weight[1], preferred_element_type=jnp.float32).astype(
        jnp.bfloat16
    )
    stream = live_mask * (
        row_emb.astype(jnp.float32)[:, None, :] + col_emb.astype(jnp.float32)[None, :, :]
    )
    stored = []
    for layer_number in range(LAYERS):
        spacing = 2**layer_number
        normalized, inv_std, scaled = normalize(stream, norm_gain[layer_number])
        squashed = (live_mask * jax.nn.elu(scaled)).astype(jnp.bfloat16)
        padded = with_halo(squashed, (("row", 0), ("col", 1)), spacing)
        convolved = conv_forward(padded, conv_weight[layer_number], spacing, tile_rows, tile_cols)
        excited = jax.nn.elu(convolved).astype(jnp.bfloat16)
        update = jnp.dot(
            excited.reshape(-1, channels),
            proj_weight[layer_number],
            preferred_element_type=jnp.float32,
        ).reshape(tile_rows, tile_cols, channels)
        stored.append((stream, padded, convolved, excited))
        stream = stream + live_mask * update
    pair_output = stream.astype(jnp.bfloat16)
    grad_scale = 1.0 / residues
    back_grad = pair_cotangent.astype(jnp.float32)
    gain_terms = [None] * LAYERS
    conv_terms = [None] * LAYERS
    proj_terms = [None] * LAYERS
    for layer_number in reversed(range(LAYERS)):
        spacing = 2**layer_number
        old_stream, padded, convolved, excited = stored[layer_number]
        masked = (live_mask * back_grad).astype(jnp.bfloat16)
        flat_masked = masked.reshape(-1, channels)
        proj_term = (
            lax.dot_general(
                excited.reshape(-1, channels),
                flat_masked,
                (((0,), (0,)), ((), ())),
                preferred_element_type=jnp.float32,
            )
            * grad_scale
        )
        d_excited = jnp.dot(
            flat_masked, proj_weight[layer_number].T, preferred_element_type=jnp.float32
        ).reshape(tile_rows, tile_cols, channels)
        d_pre = (d_excited * elu_slope(convolved)).astype(jnp.bfloat16)
        conv_term = conv_weight_grad(padded, d_pre, spacing, tile_rows, tile_cols) * grad_scale
        d_padded = with_halo(d_pre, (("row", 0), ("col", 1)), spacing)
        d_squashed = conv_backward(
            d_padded, conv_weight[layer_number], spacing, tile_rows, tile_cols
        )
        normalized, inv_std, scaled = normalize(old_stream, norm_gain[layer_number])
        d_scaled = live_mask * d_squashed * elu_slope(scaled)
        gain_term = jnp.sum(d_scaled * normalized, axis=(0, 1)) * grad_scale
        d_norm = d_scaled * norm_gain[layer_number]
        back_grad = back_grad + inv_std * (
            d_norm
            - jnp.mean(d_norm, axis=-1, keepdims=True)
            - normalized * jnp.mean(d_norm * normalized, axis=-1, keepdims=True)
        )
        gain_terms[layer_number] = gain_term
        conv_terms[layer_number] = conv_term
        proj_terms[layer_number] = proj_term
    final_masked = live_mask * back_grad
    row_totals = jnp.sum(final_masked, axis=1)
    col_totals = jnp.sum(final_masked, axis=0)
    d_row = lax.psum_scatter(row_totals, "col", scatter_dimension=0, tiled=True).astype(
        jnp.bfloat16
    )
    spread_cols = lax.dynamic_update_slice_in_dim(
        jnp.zeros((residues, channels), jnp.float32), col_totals, col_start, 0
    )
    d_col = lax.psum_scatter(spread_cols, ("row", "col"), scatter_dimension=0, tiled=True).astype(
        jnp.bfloat16
    )
    seq_grad = (
        jnp.dot(d_row, embed_weight[0].T, preferred_element_type=jnp.float32)
        + jnp.dot(d_col, embed_weight[1].T, preferred_element_type=jnp.float32)
    ) / math.sqrt(residues)
    embed_term = (
        jnp.stack(
            [
                lax.dot_general(
                    seq_feat, d_row, (((0,), (0,)), ((), ())), preferred_element_type=jnp.float32
                ),
                lax.dot_general(
                    seq_feat, d_col, (((0,), (0,)), ((), ())), preferred_element_type=jnp.float32
                ),
            ]
        )
        * grad_scale
    )
    gain_grad = jnp.stack(gain_terms)
    conv_grad = jnp.stack(conv_terms)
    proj_grad = jnp.stack(proj_terms)
    gain_grad, conv_grad, proj_grad, embed_grad = lax.psum(
        (gain_grad, conv_grad, proj_grad, embed_term), ("row", "col")
    )
    return (pair_output, seq_grad, embed_grad, gain_grad, conv_grad, proj_grad)


NT = (((1,), (1,)), ((), ()))
TN = (((0,), (0,)), ((), ()))
NN = (((1,), (0,)), ((), ()))


def dot(a, b, dims):
    return lax.dot_general(a, b, dims, preferred_element_type=jnp.float32)


def most_live(residues):
    return residues - residues // 4


CHUNK = 8


def mix_parts(height):
    return [slice(0, height)]


def in_hbm(x):
    return pltpu.with_memory_space_constraint(x, pltpu.HBM)


def pack_kernel(seq_ref, tile_ref, out_ref):
    rows, channels = out_ref.shape
    tile = tile_ref.shape[0] * tile_ref.shape[1]
    out_ref[:tile, :] = tile_ref[...].reshape(tile, channels)
    seq = seq_ref[...].astype(jnp.float32)
    own, features = seq.shape
    parts = [seq[:, k : k + channels] for k in range(0, features, channels)]
    parts.append(jnp.zeros((rows - tile - own * len(parts), channels), jnp.float32))
    out_ref[tile:, :] = jnp.concatenate(parts, axis=0).astype(out_ref.dtype)


def setup_kernel(*refs):
    lengths_hbm, refs = refs[0], refs[1:]
    half = (len(refs) - 3) // 2
    live_ref, lengths, sem = refs[half], refs[-2], refs[-1]
    copies = [
        pltpu.make_async_copy(refs[k], refs[half + 1 + k], sem.at[k]) for k in range(half)
    ]
    count_copy = pltpu.make_async_copy(lengths_hbm, lengths, sem.at[half])
    for copy in [count_copy] + copies:
        copy.start()
    pixel = jnp.maximum(
        lax.broadcasted_iota(jnp.int32, live_ref.shape, 0),
        lax.broadcasted_iota(jnp.int32, live_ref.shape, 1),
    )
    count_copy.wait()
    live_ref[...] = (pixel < lengths[0]).astype(live_ref.dtype)
    for copy in copies:
        copy.wait()


def block_kernel(grid_rows, grid_cols, *refs):
    pieces, refs = refs[:2], refs[2:]
    live, embed, gains, weights, proj = refs[:5]
    (pair_hbm, seq_grad_hbm, embed_grad_hbm, gain_grad_hbm, conv_grad_hbm, proj_grad_hbm) = refs[5:11]
    (
        stream,
        back,
        shifted,
        taps,
        mixed,
        normed,
        inv,
        slope,
        squashed,
        conv_slope,
        excited,
        masked,
        spread,
        seq_lo,
        seq_hi,
        pair_ref,
        seq_grad_ref,
        embed_grad_ref,
        gain_grad_ref,
        conv_grad,
        proj_grad_ref,
        sem,
        grad_sem,
    ) = refs[11:]
    tile_rows, tile_cols, channels = pair_ref.shape
    residues = tile_rows * grid_rows
    own = seq_grad_ref.shape[0]
    height = most_live(residues)
    count = height * height
    margin = 2 ** (LAYERS - 1)
    pad = margin * height
    chunks = [slice(k * CHUNK, (k + 1) * CHUNK) for k in range(height // CHUNK)]
    row, col = lax.axis_index("row"), lax.axis_index("col")
    stores = []

    def store(source, target, semaphore):
        copy = pltpu.make_async_copy(source, target, semaphore)
        copy.start()
        stores.append(copy)

    stream[...] = jnp.zeros_like(stream)
    shifted[...] = jnp.zeros_like(shifted)
    for ref in (taps, mixed):
        ref[:pad, :] = jnp.zeros((pad, ref.shape[1]), ref.dtype)
        ref[pad + count :, :] = jnp.zeros((pad, ref.shape[1]), ref.dtype)

    piece_rows = pieces[0].shape[0] // (2 * grid_rows)
    tile = tile_rows * tile_cols
    for step_col in range(grid_cols):
        source_col = lax.bitwise_xor(col, step_col)
        for step_row in range(grid_rows):
            source_row = lax.rem(row + grid_rows - step_row, grid_rows)
            first = (step_col // 2 * grid_rows + step_row) * piece_rows
            piece = pieces[step_col % 2][first : first + piece_rows, :].astype(jnp.float32)
            back[
                pl.ds(pl.multiple_of(source_row * tile_rows, tile_rows), tile_rows),
                pl.ds(pl.multiple_of(source_col * tile_cols, tile_cols), tile_cols),
                :,
            ] = piece[:tile].reshape(tile_rows, tile_cols, channels)
            owner = source_row * grid_cols + source_col
            spread[pl.ds(pl.multiple_of(owner * 8, 8), 8), :] = piece[tile : tile + 8]
    owners = grid_rows * grid_cols
    for k in range(own):
        seq_lo[pl.ds(k, owners, stride=own), :] = spread[pl.ds(k, owners, stride=8), :]
        seq_hi[pl.ds(k, owners, stride=own), :] = spread[pl.ds(own + k, owners, stride=8), :]
    seq = jnp.concatenate([seq_lo[...], seq_hi[...]], axis=1).astype(jnp.bfloat16)

    def get(ref, part):
        return ref[part, :height, :].reshape(-1, channels)

    def put(ref, part, value):
        ref[part, :height, :] = value.reshape(CHUNK, height, channels)

    row_emb = dot(seq, embed[0], NN).astype(jnp.bfloat16).astype(jnp.float32)
    col_emb = dot(seq, embed[1], NN).astype(jnp.bfloat16).astype(jnp.float32)
    for part in chunks:
        stream[part, :height, :] = live[part, :height, :] * (
            row_emb[part, None, :] + col_emb[None, :height, :]
        )

    def lane_mean(x):
        return jnp.mean(x, axis=-1, keepdims=True)

    def flat(part):
        return slice(part.start * height, part.stop * height)

    def moved(rows, by):
        return slice(pad + rows.start + by * height, pad + rows.stop + by * height)

    def store_shifted(part, value):
        shifted[part, margin : margin + height, :] = value.reshape(CHUNK, height, channels)

    def fill_taps(part, spacing):
        for b in (-1, 0, 1):
            start = margin + b * spacing
            value = shifted[part, start : start + height, :].reshape(-1, channels)
            taps[moved(flat(part), 0), (b + 1) * channels : (b + 2) * channels] = value.astype(
                jnp.bfloat16
            )

    def mix(part, matrix, dims):
        rows = moved(flat(part), 0)
        mixed[rows, :] = dot(taps[rows, :], matrix, dims)

    def gather_rows(part, spacing):
        return sum(
            mixed[moved(flat(part), a * spacing), (a + 1) * channels : (a + 2) * channels]
            for a in (-1, 0, 1)
        )

    def block(layer, a, b):
        first = (3 * a + b) * channels
        return weights[layer, first : first + channels, :]

    for layer in range(LAYERS):
        spacing = 2**layer
        gain = gains[layer : layer + 1, :]
        for part in chunks:
            value = get(stream, part)
            centred = value - lane_mean(value)
            inv_std = lax.rsqrt(lane_mean(centred * centred) + eps)
            normalized = centred * inv_std
            scaled = normalized * gain
            decay = jnp.exp(jnp.minimum(scaled, 0.0))
            activated = jnp.maximum(scaled, 0.0) + (decay - 1.0)
            rows = flat(part)
            normed[layer, rows, :] = normalized
            inv[layer, rows, :] = jnp.broadcast_to(inv_std, normalized.shape)
            slope[layer, rows, :] = decay * get(live, part)
            store_shifted(part, activated)
            squashed[layer, rows, :] = activated.astype(jnp.bfloat16)
            fill_taps(part, spacing)
        wide = jnp.concatenate(
            [jnp.concatenate([block(layer, a, b) for b in range(3)], axis=0) for a in range(3)],
            axis=1,
        )
        for part in mix_parts(height):
            mix(part, wide, NN)
        for part in chunks:
            convolved = gather_rows(part, spacing)
            decay = jnp.exp(jnp.minimum(convolved, 0.0))
            rows = flat(part)
            conv_slope[layer, rows, :] = decay
            hidden = (jnp.maximum(convolved, 0.0) + (decay - 1.0)).astype(jnp.bfloat16)
            excited[layer, rows, :] = hidden
            update = dot(hidden, proj[layer], NN)
            put(stream, part, get(stream, part) + get(live, part) * update)

    pair_ref[...] = stream[
        pl.ds(pl.multiple_of(row * tile_rows, tile_rows), tile_rows),
        pl.ds(pl.multiple_of(col * tile_cols, tile_cols), tile_cols),
        :,
    ].astype(jnp.bfloat16)
    store(pair_ref, pair_hbm, sem.at[0])

    grad_scale = 1.0 / residues
    for part in chunks:
        put(back, part, get(back, part) * get(live, part))
    for layer in reversed(range(LAYERS)):
        spacing = 2**layer
        gain = gains[layer : layer + 1, :]
        for part in chunks:
            grad = get(back, part).astype(jnp.bfloat16)
            rows = flat(part)
            masked[rows, :] = grad
            store_shifted(part, dot(grad, proj[layer], NT) * conv_slope[layer, rows, :])
            fill_taps(part, -spacing)
        wide = jnp.concatenate(
            [jnp.concatenate([block(layer, a, b) for b in range(3)], axis=1) for a in range(3)],
            axis=0,
        )
        for part in mix_parts(height):
            mix(part, wide, NT)
        gain_total = jnp.zeros((1, channels), jnp.float32)
        for part in chunks:
            rows = flat(part)
            normalized = normed[layer, rows, :]
            d_scaled = gather_rows(part, -spacing) * slope[layer, rows, :]
            gain_total = gain_total + jnp.sum(d_scaled * normalized, axis=0, keepdims=True)
            d_norm = d_scaled * gain
            delta = inv[layer, rows, :] * (
                d_norm - lane_mean(d_norm) - normalized * lane_mean(d_norm * normalized)
            )
            put(back, part, get(back, part) + delta)
        gain_grad_ref[layer : layer + 1, :] = gain_total * grad_scale
        proj_grad_ref[layer] = dot(excited[layer], masked[...], TN) * grad_scale
        every = slice(0, count)
        for a in (-1, 0, 1):
            part_grad = dot(squashed[layer], taps[moved(every, -a * spacing), :], TN) * grad_scale
            for b in range(3):
                conv_grad[layer, 3 * (a + 1) + b] = part_grad[:, b * channels : (b + 1) * channels]
        store(conv_grad.at[layer], conv_grad_hbm.at[layer], grad_sem.at[0, layer])
        store(proj_grad_ref.at[layer], proj_grad_hbm.at[layer], grad_sem.at[1, layer])

    final = back[:height, :height, :]
    rest = jnp.zeros((residues - height, channels), jnp.float32)
    d_row = jnp.concatenate([jnp.sum(final, axis=1), rest], axis=0).astype(jnp.bfloat16)
    d_col = jnp.concatenate([jnp.sum(final, axis=0), rest], axis=0).astype(jnp.bfloat16)
    embed_grad_ref[0] = dot(seq, d_row, TN) * grad_scale
    embed_grad_ref[1] = dot(seq, d_col, TN) * grad_scale
    store(gain_grad_ref, gain_grad_hbm, sem.at[1])
    store(embed_grad_ref, embed_grad_hbm, sem.at[2])
    seq_grad = (dot(d_row, embed[0], NT) + dot(d_col, embed[1], NT)) / math.sqrt(residues)
    first = own * (row * grid_cols + col)
    for k in range(own):
        chosen = lax.broadcasted_iota(jnp.int32, seq_grad.shape, 0) == first + k
        seq_grad_ref[k : k + 1, :] = jnp.sum(
            jnp.where(chosen, seq_grad, 0.0), axis=0, keepdims=True
        )
    store(seq_grad_ref, seq_grad_hbm, sem.at[3])
    for copy in stores:
        copy.wait()


def replicated_body(
    seq_feat, lengths, embed_weight, norm_gain, conv_weight, proj_weight, pair_cotangent
):
    tile_rows, tile_cols, channels = pair_cotangent.shape
    grid_rows, grid_cols = lax.axis_size("row"), lax.axis_size("col")
    residues = tile_rows * grid_rows
    height = most_live(residues)
    margin = 2 ** (LAYERS - 1)
    own, features = seq_feat.shape
    f32, bf16 = jnp.float32, jnp.bfloat16
    vmem = pl.BlockSpec(memory_space=pltpu.VMEM)
    hbm = pl.BlockSpec(memory_space=pltpu.HBM)
    square = (residues, residues, channels)
    payload = pl.pallas_call(
        pack_kernel,
        out_shape=pltpu.VMEM((tile_rows * tile_cols + 8, channels), bf16),
    )(in_hbm(seq_feat), in_hbm(pair_cotangent))
    payload = lax.optimization_barrier(payload)
    held = (
        embed_weight,
        norm_gain,
        conv_weight.reshape(LAYERS, 9 * channels, channels),
        proj_weight,
    )
    live, *held = pl.pallas_call(
        setup_kernel,
        out_shape=[pltpu.VMEM(square, f32)] + [pltpu.VMEM(x.shape, x.dtype) for x in held],
        in_specs=[hbm] * (1 + len(held)),
        scratch_shapes=[
            pltpu.SMEM(lengths.shape, jnp.int32),
            pltpu.SemaphoreType.DMA((1 + len(held),)),
        ],
        cost_estimate=pl.CostEstimate(flops=0, bytes_accessed=4 * 2**20, transcendentals=0),
    )(in_hbm(lengths), *[in_hbm(x) for x in held])

    def swap(x, axis, count, bit):
        return lax.ppermute(x, axis, [(i, i ^ bit) for i in range(count)])

    def rotate(x, axis, count, step):
        return lax.ppermute(x, axis, [(i, (i + step) % count) for i in range(count)])

    columns = [payload] + [rotate(payload, "row", grid_rows, k) for k in range(1, grid_rows)]
    columns, live, held = lax.optimization_barrier((columns, live, held))
    column = lax.optimization_barrier(jnp.concatenate(columns, axis=0))
    chip = jnp.concatenate([column, swap(column, "col", grid_cols, 2)], axis=0)
    chip = lax.optimization_barrier(chip)
    pieces = [chip, swap(chip, "col", grid_cols, 1)]
    count = height * height
    edge = margin * height
    saved = (LAYERS, count, channels)
    results = (
        jax.ShapeDtypeStruct((tile_rows, tile_cols, channels), bf16),
        jax.ShapeDtypeStruct((own, features), f32),
        jax.ShapeDtypeStruct((2, features, channels), f32),
        jax.ShapeDtypeStruct((LAYERS, channels), f32),
        jax.ShapeDtypeStruct((LAYERS, 9, channels, channels), f32),
        jax.ShapeDtypeStruct((LAYERS, channels, channels), f32),
    )
    outs = pl.pallas_call(
        functools.partial(block_kernel, grid_rows, grid_cols),
        out_shape=results,
        in_specs=[vmem] * 7,
        out_specs=(hbm,) * len(results),
        scratch_shapes=[
            pltpu.VMEM(square, f32),
            pltpu.VMEM(square, f32),
            pltpu.VMEM((height, height + 2 * margin, channels), f32),
            pltpu.VMEM((count + 2 * edge, 3 * channels), bf16),
            pltpu.VMEM((count + 2 * edge, 3 * channels), f32),
            pltpu.VMEM(saved, f32),
            pltpu.VMEM(saved, f32),
            pltpu.VMEM(saved, f32),
            pltpu.VMEM(saved, bf16),
            pltpu.VMEM(saved, f32),
            pltpu.VMEM(saved, bf16),
            pltpu.VMEM((count, channels), bf16),
            pltpu.VMEM((8 * grid_rows * grid_cols, channels), f32),
            pltpu.VMEM((residues, channels), f32),
            pltpu.VMEM((residues, channels), f32),
            *[pltpu.VMEM(x.shape, x.dtype) for x in results],
            pltpu.SemaphoreType.DMA((4,)),
            pltpu.SemaphoreType.DMA((2, LAYERS)),
        ],
        compiler_params=pltpu.CompilerParams(vmem_limit_bytes=40 * 1024 * 1024),
    )(*pieces, live, *held)
    pair_output, seq_grad, embed_grad, gain_grad, conv_grad, proj_grad = outs
    return (
        pair_output,
        seq_grad,
        embed_grad,
        gain_grad,
        conv_grad.reshape(LAYERS, 3, 3, channels, channels),
        proj_grad,
    )


def body(seq_feat, lengths, embed_weight, norm_gain, conv_weight, proj_weight, pair_cotangent):
    residues = pair_cotangent.shape[0] * lax.axis_size("row")
    plan = replicated_body if residues <= 32 else tiled_body
    return plan(
        seq_feat, lengths, embed_weight, norm_gain, conv_weight, proj_weight, pair_cotangent
    )


def solution(mesh):
    placed = (
        P(("groups", "row", "col"), None),
        P("groups"),
        P(),
        P(),
        P(),
        P(),
        P(("groups", "row"), "col", None),
    )
    return jax.shard_map(
        body,
        mesh=mesh,
        in_specs=placed,
        out_specs=(
            P(("groups", "row"), "col", None),
            P(("groups", "row", "col"), None),
            P("groups", None, None),
            P("groups", None),
            P("groups", None, None, None, None),
            P("groups", None, None),
        ),
        check_vma=False,
    )
```

```python
import functools
import math

import jax
import jax.numpy as jnp
from jax import lax
from jax.experimental import pallas as pl
from jax.experimental.pallas import tpu as pltpu
from jax.sharding import PartitionSpec as P

LAYERS = 4


eps = 1e-05


def with_halo(x, sides, width):
    for axis, dim in sides:
        count, length = (lax.axis_size(axis), x.shape[dim])
        up = [(i, (i + 1) % count) for i in range(count - 1)]
        down = [(j, i) for i, j in up]
        last = lax.slice_in_dim(x, length - width, length, axis=dim)
        first = lax.slice_in_dim(x, 0, width, axis=dim)
        before = lax.ppermute(last, axis, up)
        after = lax.ppermute(first, axis, down)
        x = jnp.concatenate([before, x, after], axis=dim)
    return x


def elu_slope(values):
    return jnp.where(values > 0, 1.0, jnp.exp(jnp.minimum(values, 0.0)))


def normalize(stream, gain_row):
    average = jnp.mean(stream, axis=-1, keepdims=True)
    centred = stream - average
    variance = jnp.mean(centred * centred, axis=-1, keepdims=True)
    inv_std = lax.rsqrt(variance + eps)
    normalized = centred * inv_std
    return (normalized, inv_std, normalized * gain_row)


def conv_forward(padded, weight, spacing, height, width):
    channels = padded.shape[-1]
    summed = jnp.zeros((height * width, weight.shape[-1]), jnp.float32)
    for tap_row in range(3):
        for tap_col in range(3):
            window = padded[
                tap_row * spacing : tap_row * spacing + height,
                tap_col * spacing : tap_col * spacing + width,
                :,
            ]
            summed = summed + jnp.dot(
                window.reshape(height * width, channels),
                weight[tap_row, tap_col],
                preferred_element_type=jnp.float32,
            )
    return summed.reshape(height, width, -1)


def conv_backward(padded, weight, spacing, height, width):
    channels = padded.shape[-1]
    summed = jnp.zeros((height * width, weight.shape[-2]), jnp.float32)
    for tap_row in range(3):
        for tap_col in range(3):
            start_row = (2 - tap_row) * spacing
            start_col = (2 - tap_col) * spacing
            window = padded[start_row : start_row + height, start_col : start_col + width, :]
            summed = summed + jnp.dot(
                window.reshape(height * width, channels),
                weight[tap_row, tap_col].T,
                preferred_element_type=jnp.float32,
            )
    return summed.reshape(height, width, -1)


def conv_weight_grad(padded, grad_tile, spacing, height, width):
    channels = padded.shape[-1]
    flat_grad = grad_tile.reshape(height * width, -1)
    terms = []
    for tap_row in range(3):
        row_terms = []
        for tap_col in range(3):
            window = padded[
                tap_row * spacing : tap_row * spacing + height,
                tap_col * spacing : tap_col * spacing + width,
                :,
            ]
            row_terms.append(
                lax.dot_general(
                    window.reshape(height * width, channels),
                    flat_grad,
                    (((0,), (0,)), ((), ())),
                    preferred_element_type=jnp.float32,
                )
            )
        terms.append(jnp.stack(row_terms))
    return jnp.stack(terms)


def tiled_body(seq_feat, lengths, embed_weight, norm_gain, conv_weight, proj_weight, pair_cotangent):
    tile_rows = pair_cotangent.shape[0]
    tile_cols = pair_cotangent.shape[1]
    channels = pair_cotangent.shape[2]
    residues = tile_rows * lax.axis_size("row")
    row_start = lax.axis_index("row") * tile_rows
    col_start = lax.axis_index("col") * tile_cols
    row_live = (row_start + jnp.arange(tile_rows, dtype=jnp.int32) < lengths[0]).astype(jnp.float32)
    col_live = (col_start + jnp.arange(tile_cols, dtype=jnp.int32) < lengths[0]).astype(jnp.float32)
    live_mask = row_live[:, None, None] * col_live[None, :, None]
    gathered = lax.all_gather(seq_feat, ("row", "col"), axis=0, tiled=True)
    row_part = lax.dynamic_slice_in_dim(gathered, row_start, tile_rows, 0)
    col_part = lax.dynamic_slice_in_dim(gathered, col_start, tile_cols, 0)
    row_emb = jnp.dot(row_part, embed_weight[0], preferred_element_type=jnp.float32).astype(
        jnp.bfloat16
    )
    col_emb = jnp.dot(col_part, embed_weight[1], preferred_element_type=jnp.float32).astype(
        jnp.bfloat16
    )
    stream = live_mask * (
        row_emb.astype(jnp.float32)[:, None, :] + col_emb.astype(jnp.float32)[None, :, :]
    )
    stored = []
    for layer_number in range(LAYERS):
        spacing = 2**layer_number
        normalized, inv_std, scaled = normalize(stream, norm_gain[layer_number])
        squashed = (live_mask * jax.nn.elu(scaled)).astype(jnp.bfloat16)
        padded = with_halo(squashed, (("row", 0), ("col", 1)), spacing)
        convolved = conv_forward(padded, conv_weight[layer_number], spacing, tile_rows, tile_cols)
        excited = jax.nn.elu(convolved).astype(jnp.bfloat16)
        update = jnp.dot(
            excited.reshape(-1, channels),
            proj_weight[layer_number],
            preferred_element_type=jnp.float32,
        ).reshape(tile_rows, tile_cols, channels)
        stored.append((stream, padded, convolved, excited))
        stream = stream + live_mask * update
    pair_output = stream.astype(jnp.bfloat16)
    grad_scale = 1.0 / residues
    back_grad = pair_cotangent.astype(jnp.float32)
    gain_terms = [None] * LAYERS
    conv_terms = [None] * LAYERS
    proj_terms = [None] * LAYERS
    for layer_number in reversed(range(LAYERS)):
        spacing = 2**layer_number
        old_stream, padded, convolved, excited = stored[layer_number]
        masked = (live_mask * back_grad).astype(jnp.bfloat16)
        flat_masked = masked.reshape(-1, channels)
        proj_term = (
            lax.dot_general(
                excited.reshape(-1, channels),
                flat_masked,
                (((0,), (0,)), ((), ())),
                preferred_element_type=jnp.float32,
            )
            * grad_scale
        )
        d_excited = jnp.dot(
            flat_masked, proj_weight[layer_number].T, preferred_element_type=jnp.float32
        ).reshape(tile_rows, tile_cols, channels)
        d_pre = (d_excited * elu_slope(convolved)).astype(jnp.bfloat16)
        conv_term = conv_weight_grad(padded, d_pre, spacing, tile_rows, tile_cols) * grad_scale
        d_padded = with_halo(d_pre, (("row", 0), ("col", 1)), spacing)
        d_squashed = conv_backward(
            d_padded, conv_weight[layer_number], spacing, tile_rows, tile_cols
        )
        normalized, inv_std, scaled = normalize(old_stream, norm_gain[layer_number])
        d_scaled = live_mask * d_squashed * elu_slope(scaled)
        gain_term = jnp.sum(d_scaled * normalized, axis=(0, 1)) * grad_scale
        d_norm = d_scaled * norm_gain[layer_number]
        back_grad = back_grad + inv_std * (
            d_norm
            - jnp.mean(d_norm, axis=-1, keepdims=True)
            - normalized * jnp.mean(d_norm * normalized, axis=-1, keepdims=True)
        )
        gain_terms[layer_number] = gain_term
        conv_terms[layer_number] = conv_term
        proj_terms[layer_number] = proj_term
    final_masked = live_mask * back_grad
    row_totals = jnp.sum(final_masked, axis=1)
    col_totals = jnp.sum(final_masked, axis=0)
    d_row = lax.psum_scatter(row_totals, "col", scatter_dimension=0, tiled=True).astype(
        jnp.bfloat16
    )
    spread_cols = lax.dynamic_update_slice_in_dim(
        jnp.zeros((residues, channels), jnp.float32), col_totals, col_start, 0
    )
    d_col = lax.psum_scatter(spread_cols, ("row", "col"), scatter_dimension=0, tiled=True).astype(
        jnp.bfloat16
    )
    seq_grad = (
        jnp.dot(d_row, embed_weight[0].T, preferred_element_type=jnp.float32)
        + jnp.dot(d_col, embed_weight[1].T, preferred_element_type=jnp.float32)
    ) / math.sqrt(residues)
    embed_term = (
        jnp.stack(
            [
                lax.dot_general(
                    seq_feat, d_row, (((0,), (0,)), ((), ())), preferred_element_type=jnp.float32
                ),
                lax.dot_general(
                    seq_feat, d_col, (((0,), (0,)), ((), ())), preferred_element_type=jnp.float32
                ),
            ]
        )
        * grad_scale
    )
    gain_grad = jnp.stack(gain_terms)
    conv_grad = jnp.stack(conv_terms)
    proj_grad = jnp.stack(proj_terms)
    gain_grad, conv_grad, proj_grad, embed_grad = lax.psum(
        (gain_grad, conv_grad, proj_grad, embed_term), ("row", "col")
    )
    return (pair_output, seq_grad, embed_grad, gain_grad, conv_grad, proj_grad)


NT = (((1,), (1,)), ((), ()))
TN = (((0,), (0,)), ((), ()))
NN = (((1,), (0,)), ((), ()))


def dot(a, b, dims):
    return lax.dot_general(a, b, dims, preferred_element_type=jnp.float32)


def most_live(residues):
    return residues - residues // 4


CHUNK = 8


def mix_parts(height):
    return [slice(0, height)]


def in_hbm(x):
    return pltpu.with_memory_space_constraint(x, pltpu.HBM)


def pack_kernel(seq_ref, tile_ref, out_ref):
    rows, channels = out_ref.shape
    tile = tile_ref.shape[0] * tile_ref.shape[1]
    out_ref[:tile, :] = tile_ref[...].reshape(tile, channels)
    seq = seq_ref[...].astype(jnp.float32)
    own, features = seq.shape
    parts = [seq[:, k : k + channels] for k in range(0, features, channels)]
    parts.append(jnp.zeros((rows - tile - own * len(parts), channels), jnp.float32))
    out_ref[tile:, :] = jnp.concatenate(parts, axis=0).astype(out_ref.dtype)


def setup_kernel(*refs):
    lengths_hbm, refs = refs[0], refs[1:]
    half = (len(refs) - 3) // 2
    live_ref, lengths, sem = refs[half], refs[-2], refs[-1]
    copies = [
        pltpu.make_async_copy(refs[k], refs[half + 1 + k], sem.at[k]) for k in range(half)
    ]
    count_copy = pltpu.make_async_copy(lengths_hbm, lengths, sem.at[half])
    for copy in [count_copy] + copies:
        copy.start()
    pixel = jnp.maximum(
        lax.broadcasted_iota(jnp.int32, live_ref.shape, 0),
        lax.broadcasted_iota(jnp.int32, live_ref.shape, 1),
    )
    count_copy.wait()
    live_ref[...] = (pixel < lengths[0]).astype(live_ref.dtype)
    for copy in copies:
        copy.wait()


def block_kernel(grid_rows, grid_cols, *refs):
    pieces, refs = refs[:2], refs[2:]
    live, embed, gains, weights, proj = refs[:5]
    (pair_hbm, seq_grad_hbm, embed_grad_hbm, gain_grad_hbm, conv_grad_hbm, proj_grad_hbm) = refs[5:11]
    (
        stream,
        back,
        shifted,
        taps,
        mixed,
        normed,
        inv,
        slope,
        squashed,
        conv_slope,
        excited,
        masked,
        spread,
        seq_lo,
        seq_hi,
        pair_ref,
        seq_grad_ref,
        embed_grad_ref,
        gain_grad_ref,
        conv_grad,
        proj_grad_ref,
        sem,
        grad_sem,
    ) = refs[11:]
    tile_rows, tile_cols, channels = pair_ref.shape
    residues = tile_rows * grid_rows
    own = seq_grad_ref.shape[0]
    height = most_live(residues)
    count = height * height
    margin = 2 ** (LAYERS - 1)
    pad = margin * height
    chunks = [slice(k * CHUNK, (k + 1) * CHUNK) for k in range(height // CHUNK)]
    row, col = lax.axis_index("row"), lax.axis_index("col")
    stores = []

    def store(source, target, semaphore):
        copy = pltpu.make_async_copy(source, target, semaphore)
        copy.start()
        stores.append(copy)

    stream[...] = jnp.zeros_like(stream)
    shifted[...] = jnp.zeros_like(shifted)
    for ref in (taps, mixed):
        ref[:pad, :] = jnp.zeros((pad, ref.shape[1]), ref.dtype)
        ref[pad + count :, :] = jnp.zeros((pad, ref.shape[1]), ref.dtype)

    piece_rows = pieces[0].shape[0] // (2 * grid_rows)
    tile = tile_rows * tile_cols
    for step_col in range(grid_cols):
        source_col = lax.bitwise_xor(col, step_col)
        for step_row in range(grid_rows):
            source_row = lax.rem(row + step_row, grid_rows)
            first = (step_col // 2 * grid_rows + step_row) * piece_rows
            piece = pieces[step_col % 2][first : first + piece_rows, :].astype(jnp.float32)
            back[
                pl.ds(pl.multiple_of(source_row * tile_rows, tile_rows), tile_rows),
                pl.ds(pl.multiple_of(source_col * tile_cols, tile_cols), tile_cols),
                :,
            ] = piece[:tile].reshape(tile_rows, tile_cols, channels)
            owner = source_row * grid_cols + source_col
            spread[pl.ds(pl.multiple_of(owner * 8, 8), 8), :] = piece[tile : tile + 8]
    owners = grid_rows * grid_cols
    for k in range(own):
        seq_lo[pl.ds(k, owners, stride=own), :] = spread[pl.ds(k, owners, stride=8), :]
        seq_hi[pl.ds(k, owners, stride=own), :] = spread[pl.ds(own + k, owners, stride=8), :]
    seq = jnp.concatenate([seq_lo[...], seq_hi[...]], axis=1).astype(jnp.bfloat16)

    def get(ref, part):
        return ref[part, :height, :].reshape(-1, channels)

    def put(ref, part, value):
        ref[part, :height, :] = value.reshape(CHUNK, height, channels)

    row_emb = dot(seq, embed[0], NN).astype(jnp.bfloat16).astype(jnp.float32)
    col_emb = dot(seq, embed[1], NN).astype(jnp.bfloat16).astype(jnp.float32)
    for part in chunks:
        stream[part, :height, :] = live[part, :height, :] * (
            row_emb[part, None, :] + col_emb[None, :height, :]
        )

    def lane_mean(x):
        return jnp.mean(x, axis=-1, keepdims=True)

    def flat(part):
        return slice(part.start * height, part.stop * height)

    def moved(rows, by):
        return slice(pad + rows.start + by * height, pad + rows.stop + by * height)

    def store_shifted(part, value):
        shifted[part, margin : margin + height, :] = value.reshape(CHUNK, height, channels)

    def fill_taps(part, spacing):
        for b in (-1, 0, 1):
            start = margin + b * spacing
            value = shifted[part, start : start + height, :].reshape(-1, channels)
            taps[moved(flat(part), 0), (b + 1) * channels : (b + 2) * channels] = value.astype(
                jnp.bfloat16
            )

    def mix(part, matrix, dims):
        rows = moved(flat(part), 0)
        mixed[rows, :] = dot(taps[rows, :], matrix, dims)

    def gather_rows(part, spacing):
        return sum(
            mixed[moved(flat(part), a * spacing), (a + 1) * channels : (a + 2) * channels]
            for a in (-1, 0, 1)
        )

    def block(layer, a, b):
        first = (3 * a + b) * channels
        return weights[layer, first : first + channels, :]

    for layer in range(LAYERS):
        spacing = 2**layer
        gain = gains[layer : layer + 1, :]
        for part in chunks:
            value = get(stream, part)
            centred = value - lane_mean(value)
            inv_std = lax.rsqrt(lane_mean(centred * centred) + eps)
            normalized = centred * inv_std
            scaled = normalized * gain
            decay = jnp.exp(jnp.minimum(scaled, 0.0))
            activated = jnp.maximum(scaled, 0.0) + (decay - 1.0)
            rows = flat(part)
            normed[layer, rows, :] = normalized
            inv[layer, rows, :] = jnp.broadcast_to(inv_std, normalized.shape)
            slope[layer, rows, :] = decay * get(live, part)
            store_shifted(part, activated)
            squashed[layer, rows, :] = activated.astype(jnp.bfloat16)
            fill_taps(part, spacing)
        wide = jnp.concatenate(
            [jnp.concatenate([block(layer, a, b) for b in range(3)], axis=0) for a in range(3)],
            axis=1,
        )
        for part in mix_parts(height):
            mix(part, wide, NN)
        for part in chunks:
            convolved = gather_rows(part, spacing)
            decay = jnp.exp(jnp.minimum(convolved, 0.0))
            rows = flat(part)
            conv_slope[layer, rows, :] = decay
            hidden = (jnp.maximum(convolved, 0.0) + (decay - 1.0)).astype(jnp.bfloat16)
            excited[layer, rows, :] = hidden
            update = dot(hidden, proj[layer], NN)
            put(stream, part, get(stream, part) + get(live, part) * update)

    pair_ref[...] = stream[
        pl.ds(pl.multiple_of(row * tile_rows, tile_rows), tile_rows),
        pl.ds(pl.multiple_of(col * tile_cols, tile_cols), tile_cols),
        :,
    ].astype(jnp.bfloat16)
    store(pair_ref, pair_hbm, sem.at[0])

    grad_scale = 1.0 / residues
    for part in chunks:
        put(back, part, get(back, part) * get(live, part))
    for layer in reversed(range(LAYERS)):
        spacing = 2**layer
        gain = gains[layer : layer + 1, :]
        for part in chunks:
            grad = get(back, part).astype(jnp.bfloat16)
            rows = flat(part)
            masked[rows, :] = grad
            store_shifted(part, dot(grad, proj[layer], NT) * conv_slope[layer, rows, :])
            fill_taps(part, -spacing)
        wide = jnp.concatenate(
            [jnp.concatenate([block(layer, a, b) for b in range(3)], axis=1) for a in range(3)],
            axis=0,
        )
        for part in mix_parts(height):
            mix(part, wide, NT)
        gain_total = jnp.zeros((1, channels), jnp.float32)
        for part in chunks:
            rows = flat(part)
            normalized = normed[layer, rows, :]
            d_scaled = gather_rows(part, -spacing) * slope[layer, rows, :]
            gain_total = gain_total + jnp.sum(d_scaled * normalized, axis=0, keepdims=True)
            d_norm = d_scaled * gain
            delta = inv[layer, rows, :] * (
                d_norm - lane_mean(d_norm) - normalized * lane_mean(d_norm * normalized)
            )
            put(back, part, get(back, part) + delta)
        gain_grad_ref[layer : layer + 1, :] = gain_total * grad_scale
        proj_grad_ref[layer] = dot(excited[layer], masked[...], TN) * grad_scale
        every = slice(0, count)
        for a in (-1, 0, 1):
            part_grad = dot(squashed[layer], taps[moved(every, -a * spacing), :], TN) * grad_scale
            for b in range(3):
                conv_grad[layer, 3 * (a + 1) + b] = part_grad[:, b * channels : (b + 1) * channels]
        store(conv_grad.at[layer], conv_grad_hbm.at[layer], grad_sem.at[0, layer])
        store(proj_grad_ref.at[layer], proj_grad_hbm.at[layer], grad_sem.at[1, layer])

    final = back[:height, :height, :]
    rest = jnp.zeros((residues - height, channels), jnp.float32)
    d_row = jnp.concatenate([jnp.sum(final, axis=1), rest], axis=0).astype(jnp.bfloat16)
    d_col = jnp.concatenate([jnp.sum(final, axis=0), rest], axis=0).astype(jnp.bfloat16)
    embed_grad_ref[0] = dot(seq, d_row, TN) * grad_scale
    embed_grad_ref[1] = dot(seq, d_col, TN) * grad_scale
    store(gain_grad_ref, gain_grad_hbm, sem.at[1])
    store(embed_grad_ref, embed_grad_hbm, sem.at[2])
    seq_grad = (dot(d_row, embed[0], NT) + dot(d_col, embed[1], NT)) / math.sqrt(residues)
    first = own * (row * grid_cols + col)
    for k in range(own):
        chosen = lax.broadcasted_iota(jnp.int32, seq_grad.shape, 0) == first + k
        seq_grad_ref[k : k + 1, :] = jnp.sum(
            jnp.where(chosen, seq_grad, 0.0), axis=0, keepdims=True
        )
    store(seq_grad_ref, seq_grad_hbm, sem.at[3])
    for copy in stores:
        copy.wait()


def replicated_body(
    seq_feat, lengths, embed_weight, norm_gain, conv_weight, proj_weight, pair_cotangent
):
    tile_rows, tile_cols, channels = pair_cotangent.shape
    grid_rows, grid_cols = lax.axis_size("row"), lax.axis_size("col")
    residues = tile_rows * grid_rows
    height = most_live(residues)
    margin = 2 ** (LAYERS - 1)
    own, features = seq_feat.shape
    f32, bf16 = jnp.float32, jnp.bfloat16
    vmem = pl.BlockSpec(memory_space=pltpu.VMEM)
    hbm = pl.BlockSpec(memory_space=pltpu.HBM)
    square = (residues, residues, channels)
    payload = pl.pallas_call(
        pack_kernel,
        out_shape=pltpu.VMEM((tile_rows * tile_cols + 8, channels), bf16),
    )(in_hbm(seq_feat), in_hbm(pair_cotangent))
    payload = lax.optimization_barrier(payload)
    def swap(x, axis, count, bit):
        return lax.ppermute(x, axis, [(i, i ^ bit) for i in range(count)])

    def rotate(x, axis, count, step):
        return lax.ppermute(x, axis, [(i, (i + step) % count) for i in range(count)])

    turns = [rotate(payload, "row", grid_rows, k) for k in reversed(range(1, grid_rows))]
    column = lax.optimization_barrier(jnp.concatenate([payload] + turns, axis=0))
    column, lengths = lax.optimization_barrier((column, lengths))
    held = (
        embed_weight,
        norm_gain,
        conv_weight.reshape(LAYERS, 9 * channels, channels),
        proj_weight,
    )
    live, *held = pl.pallas_call(
        setup_kernel,
        out_shape=[pltpu.VMEM(square, f32)] + [pltpu.VMEM(x.shape, x.dtype) for x in held],
        in_specs=[hbm] * (1 + len(held)),
        scratch_shapes=[
            pltpu.SMEM(lengths.shape, jnp.int32),
            pltpu.SemaphoreType.DMA((1 + len(held),)),
        ],
        cost_estimate=pl.CostEstimate(flops=0, bytes_accessed=4 * 2**20, transcendentals=0),
    )(in_hbm(lengths), *[in_hbm(x) for x in held])

    chip = [column, swap(column, "col", grid_cols, 2)]
    chip, live, held = lax.optimization_barrier((chip, live, held))
    chip = lax.optimization_barrier(jnp.concatenate(chip, axis=0))
    pieces = [chip, swap(chip, "col", grid_cols, 1)]
    count = height * height
    edge = margin * height
    saved = (LAYERS, count, channels)
    results = (
        jax.ShapeDtypeStruct((tile_rows, tile_cols, channels), bf16),
        jax.ShapeDtypeStruct((own, features), f32),
        jax.ShapeDtypeStruct((2, features, channels), f32),
        jax.ShapeDtypeStruct((LAYERS, channels), f32),
        jax.ShapeDtypeStruct((LAYERS, 9, channels, channels), f32),
        jax.ShapeDtypeStruct((LAYERS, channels, channels), f32),
    )
    outs = pl.pallas_call(
        functools.partial(block_kernel, grid_rows, grid_cols),
        out_shape=results,
        in_specs=[vmem] * 7,
        out_specs=(hbm,) * len(results),
        scratch_shapes=[
            pltpu.VMEM(square, f32),
            pltpu.VMEM(square, f32),
            pltpu.VMEM((height, height + 2 * margin, channels), f32),
            pltpu.VMEM((count + 2 * edge, 3 * channels), bf16),
            pltpu.VMEM((count + 2 * edge, 3 * channels), f32),
            pltpu.VMEM(saved, f32),
            pltpu.VMEM(saved, f32),
            pltpu.VMEM(saved, f32),
            pltpu.VMEM(saved, bf16),
            pltpu.VMEM(saved, f32),
            pltpu.VMEM(saved, bf16),
            pltpu.VMEM((count, channels), bf16),
            pltpu.VMEM((8 * grid_rows * grid_cols, channels), f32),
            pltpu.VMEM((residues, channels), f32),
            pltpu.VMEM((residues, channels), f32),
            *[pltpu.VMEM(x.shape, x.dtype) for x in results],
            pltpu.SemaphoreType.DMA((4,)),
            pltpu.SemaphoreType.DMA((2, LAYERS)),
        ],
        compiler_params=pltpu.CompilerParams(vmem_limit_bytes=40 * 1024 * 1024),
    )(*pieces, live, *held)
    pair_output, seq_grad, embed_grad, gain_grad, conv_grad, proj_grad = outs
    return (
        pair_output,
        seq_grad,
        embed_grad,
        gain_grad,
        conv_grad.reshape(LAYERS, 3, 3, channels, channels),
        proj_grad,
    )


def body(seq_feat, lengths, embed_weight, norm_gain, conv_weight, proj_weight, pair_cotangent):
    residues = pair_cotangent.shape[0] * lax.axis_size("row")
    plan = replicated_body if residues <= 32 else tiled_body
    return plan(
        seq_feat, lengths, embed_weight, norm_gain, conv_weight, proj_weight, pair_cotangent
    )


def solution(mesh):
    placed = (
        P(("groups", "row", "col"), None),
        P("groups"),
        P(),
        P(),
        P(),
        P(),
        P(("groups", "row"), "col", None),
    )
    return jax.shard_map(
        body,
        mesh=mesh,
        in_specs=placed,
        out_specs=(
            P(("groups", "row"), "col", None),
            P(("groups", "row", "col"), None),
            P("groups", None, None),
            P("groups", None),
            P("groups", None, None, None, None),
            P("groups", None, None),
        ),
        check_vma=False,
    )
```

```python
import functools
import math

import jax
import jax.numpy as jnp
from jax import lax
from jax.experimental import pallas as pl
from jax.experimental.pallas import tpu as pltpu
from jax.sharding import PartitionSpec as P

LAYERS = 4


eps = 1e-05


def with_halo(x, sides, width):
    for axis, dim in sides:
        count, length = (lax.axis_size(axis), x.shape[dim])
        up = [(i, (i + 1) % count) for i in range(count - 1)]
        down = [(j, i) for i, j in up]
        last = lax.slice_in_dim(x, length - width, length, axis=dim)
        first = lax.slice_in_dim(x, 0, width, axis=dim)
        before = lax.ppermute(last, axis, up)
        after = lax.ppermute(first, axis, down)
        x = jnp.concatenate([before, x, after], axis=dim)
    return x


def elu_slope(values):
    return jnp.where(values > 0, 1.0, jnp.exp(jnp.minimum(values, 0.0)))


def normalize(stream, gain_row):
    average = jnp.mean(stream, axis=-1, keepdims=True)
    centred = stream - average
    variance = jnp.mean(centred * centred, axis=-1, keepdims=True)
    inv_std = lax.rsqrt(variance + eps)
    normalized = centred * inv_std
    return (normalized, inv_std, normalized * gain_row)


def conv_forward(padded, weight, spacing, height, width):
    channels = padded.shape[-1]
    summed = jnp.zeros((height * width, weight.shape[-1]), jnp.float32)
    for tap_row in range(3):
        for tap_col in range(3):
            window = padded[
                tap_row * spacing : tap_row * spacing + height,
                tap_col * spacing : tap_col * spacing + width,
                :,
            ]
            summed = summed + jnp.dot(
                window.reshape(height * width, channels),
                weight[tap_row, tap_col],
                preferred_element_type=jnp.float32,
            )
    return summed.reshape(height, width, -1)


def conv_backward(padded, weight, spacing, height, width):
    channels = padded.shape[-1]
    summed = jnp.zeros((height * width, weight.shape[-2]), jnp.float32)
    for tap_row in range(3):
        for tap_col in range(3):
            start_row = (2 - tap_row) * spacing
            start_col = (2 - tap_col) * spacing
            window = padded[start_row : start_row + height, start_col : start_col + width, :]
            summed = summed + jnp.dot(
                window.reshape(height * width, channels),
                weight[tap_row, tap_col].T,
                preferred_element_type=jnp.float32,
            )
    return summed.reshape(height, width, -1)


def conv_weight_grad(padded, grad_tile, spacing, height, width):
    channels = padded.shape[-1]
    flat_grad = grad_tile.reshape(height * width, -1)
    terms = []
    for tap_row in range(3):
        row_terms = []
        for tap_col in range(3):
            window = padded[
                tap_row * spacing : tap_row * spacing + height,
                tap_col * spacing : tap_col * spacing + width,
                :,
            ]
            row_terms.append(
                lax.dot_general(
                    window.reshape(height * width, channels),
                    flat_grad,
                    (((0,), (0,)), ((), ())),
                    preferred_element_type=jnp.float32,
                )
            )
        terms.append(jnp.stack(row_terms))
    return jnp.stack(terms)


def tiled_body(seq_feat, lengths, embed_weight, norm_gain, conv_weight, proj_weight, pair_cotangent):
    tile_rows = pair_cotangent.shape[0]
    tile_cols = pair_cotangent.shape[1]
    channels = pair_cotangent.shape[2]
    residues = tile_rows * lax.axis_size("row")
    row_start = lax.axis_index("row") * tile_rows
    col_start = lax.axis_index("col") * tile_cols
    row_live = (row_start + jnp.arange(tile_rows, dtype=jnp.int32) < lengths[0]).astype(jnp.float32)
    col_live = (col_start + jnp.arange(tile_cols, dtype=jnp.int32) < lengths[0]).astype(jnp.float32)
    live_mask = row_live[:, None, None] * col_live[None, :, None]
    gathered = lax.all_gather(seq_feat, ("row", "col"), axis=0, tiled=True)
    row_part = lax.dynamic_slice_in_dim(gathered, row_start, tile_rows, 0)
    col_part = lax.dynamic_slice_in_dim(gathered, col_start, tile_cols, 0)
    row_emb = jnp.dot(row_part, embed_weight[0], preferred_element_type=jnp.float32).astype(
        jnp.bfloat16
    )
    col_emb = jnp.dot(col_part, embed_weight[1], preferred_element_type=jnp.float32).astype(
        jnp.bfloat16
    )
    stream = live_mask * (
        row_emb.astype(jnp.float32)[:, None, :] + col_emb.astype(jnp.float32)[None, :, :]
    )
    stored = []
    for layer_number in range(LAYERS):
        spacing = 2**layer_number
        normalized, inv_std, scaled = normalize(stream, norm_gain[layer_number])
        squashed = (live_mask * jax.nn.elu(scaled)).astype(jnp.bfloat16)
        padded = with_halo(squashed, (("row", 0), ("col", 1)), spacing)
        convolved = conv_forward(padded, conv_weight[layer_number], spacing, tile_rows, tile_cols)
        excited = jax.nn.elu(convolved).astype(jnp.bfloat16)
        update = jnp.dot(
            excited.reshape(-1, channels),
            proj_weight[layer_number],
            preferred_element_type=jnp.float32,
        ).reshape(tile_rows, tile_cols, channels)
        stored.append((stream, padded, convolved, excited))
        stream = stream + live_mask * update
    pair_output = stream.astype(jnp.bfloat16)
    grad_scale = 1.0 / residues
    back_grad = pair_cotangent.astype(jnp.float32)
    gain_terms = [None] * LAYERS
    conv_terms = [None] * LAYERS
    proj_terms = [None] * LAYERS
    for layer_number in reversed(range(LAYERS)):
        spacing = 2**layer_number
        old_stream, padded, convolved, excited = stored[layer_number]
        masked = (live_mask * back_grad).astype(jnp.bfloat16)
        flat_masked = masked.reshape(-1, channels)
        proj_term = (
            lax.dot_general(
                excited.reshape(-1, channels),
                flat_masked,
                (((0,), (0,)), ((), ())),
                preferred_element_type=jnp.float32,
            )
            * grad_scale
        )
        d_excited = jnp.dot(
            flat_masked, proj_weight[layer_number].T, preferred_element_type=jnp.float32
        ).reshape(tile_rows, tile_cols, channels)
        d_pre = (d_excited * elu_slope(convolved)).astype(jnp.bfloat16)
        conv_term = conv_weight_grad(padded, d_pre, spacing, tile_rows, tile_cols) * grad_scale
        d_padded = with_halo(d_pre, (("row", 0), ("col", 1)), spacing)
        d_squashed = conv_backward(
            d_padded, conv_weight[layer_number], spacing, tile_rows, tile_cols
        )
        normalized, inv_std, scaled = normalize(old_stream, norm_gain[layer_number])
        d_scaled = live_mask * d_squashed * elu_slope(scaled)
        gain_term = jnp.sum(d_scaled * normalized, axis=(0, 1)) * grad_scale
        d_norm = d_scaled * norm_gain[layer_number]
        back_grad = back_grad + inv_std * (
            d_norm
            - jnp.mean(d_norm, axis=-1, keepdims=True)
            - normalized * jnp.mean(d_norm * normalized, axis=-1, keepdims=True)
        )
        gain_terms[layer_number] = gain_term
        conv_terms[layer_number] = conv_term
        proj_terms[layer_number] = proj_term
    final_masked = live_mask * back_grad
    row_totals = jnp.sum(final_masked, axis=1)
    col_totals = jnp.sum(final_masked, axis=0)
    d_row = lax.psum_scatter(row_totals, "col", scatter_dimension=0, tiled=True).astype(
        jnp.bfloat16
    )
    spread_cols = lax.dynamic_update_slice_in_dim(
        jnp.zeros((residues, channels), jnp.float32), col_totals, col_start, 0
    )
    d_col = lax.psum_scatter(spread_cols, ("row", "col"), scatter_dimension=0, tiled=True).astype(
        jnp.bfloat16
    )
    seq_grad = (
        jnp.dot(d_row, embed_weight[0].T, preferred_element_type=jnp.float32)
        + jnp.dot(d_col, embed_weight[1].T, preferred_element_type=jnp.float32)
    ) / math.sqrt(residues)
    embed_term = (
        jnp.stack(
            [
                lax.dot_general(
                    seq_feat, d_row, (((0,), (0,)), ((), ())), preferred_element_type=jnp.float32
                ),
                lax.dot_general(
                    seq_feat, d_col, (((0,), (0,)), ((), ())), preferred_element_type=jnp.float32
                ),
            ]
        )
        * grad_scale
    )
    gain_grad = jnp.stack(gain_terms)
    conv_grad = jnp.stack(conv_terms)
    proj_grad = jnp.stack(proj_terms)
    gain_grad, conv_grad, proj_grad, embed_grad = lax.psum(
        (gain_grad, conv_grad, proj_grad, embed_term), ("row", "col")
    )
    return (pair_output, seq_grad, embed_grad, gain_grad, conv_grad, proj_grad)


NT = (((1,), (1,)), ((), ()))
TN = (((0,), (0,)), ((), ()))
NN = (((1,), (0,)), ((), ()))


def dot(a, b, dims):
    return lax.dot_general(a, b, dims, preferred_element_type=jnp.float32)


def most_live(residues):
    return residues - residues // 4


CHUNK = 8


def mix_parts(height):
    return [slice(0, height)]


def in_hbm(x):
    return pltpu.with_memory_space_constraint(x, pltpu.HBM)


def pack_kernel(seq_ref, tile_ref, out_ref):
    rows, channels = out_ref.shape
    tile = tile_ref.shape[0] * tile_ref.shape[1]
    out_ref[:tile, :] = tile_ref[...].reshape(tile, channels)
    seq = seq_ref[...].astype(jnp.float32)
    own, features = seq.shape
    parts = [seq[:, k : k + channels] for k in range(0, features, channels)]
    parts.append(jnp.zeros((rows - tile - own * len(parts), channels), jnp.float32))
    out_ref[tile:, :] = jnp.concatenate(parts, axis=0).astype(out_ref.dtype)


def setup_kernel(*refs):
    lengths_hbm, refs = refs[0], refs[1:]
    half = (len(refs) - 4) // 2
    live_ref, mean_ref, lengths, sem = refs[half], refs[-3], refs[-2], refs[-1]
    copies = [
        pltpu.make_async_copy(refs[k], refs[half + 1 + k], sem.at[k]) for k in range(half)
    ]
    count_copy = pltpu.make_async_copy(lengths_hbm, lengths, sem.at[half])
    for copy in [count_copy] + copies:
        copy.start()
    pixel = jnp.maximum(
        lax.broadcasted_iota(jnp.int32, live_ref.shape, 0),
        lax.broadcasted_iota(jnp.int32, live_ref.shape, 1),
    )
    count_copy.wait()
    live_ref[...] = (pixel < lengths[0]).astype(live_ref.dtype)
    for copy in copies:
        copy.wait()
    proj = refs[2 * half][...].astype(jnp.float32)
    mean = jnp.mean(proj, axis=-1, keepdims=True)
    mean_ref[...] = jnp.broadcast_to(mean, proj.shape).astype(mean_ref.dtype)


def block_kernel(grid_rows, grid_cols, *refs):
    pieces, refs = refs[:2], refs[2:]
    live, embed, gains, weights, proj, proj_mean = refs[:6]
    (pair_hbm, seq_grad_hbm, embed_grad_hbm, gain_grad_hbm, conv_grad_hbm, proj_grad_hbm) = refs[6:12]
    (
        stream,
        guess,
        back,
        shifted,
        taps,
        mixed,
        normed,
        inv,
        slope,
        squashed,
        conv_slope,
        excited,
        masked,
        spread,
        seq_lo,
        seq_hi,
        pair_ref,
        seq_grad_ref,
        embed_grad_ref,
        gain_grad_ref,
        conv_grad,
        proj_grad_ref,
        sem,
        grad_sem,
    ) = refs[12:]
    tile_rows, tile_cols, channels = pair_ref.shape
    residues = tile_rows * grid_rows
    own = seq_grad_ref.shape[0]
    height = most_live(residues)
    count = height * height
    margin = 2 ** (LAYERS - 1)
    pad = margin * height
    chunks = [slice(k * CHUNK, (k + 1) * CHUNK) for k in range(height // CHUNK)]
    row, col = lax.axis_index("row"), lax.axis_index("col")
    stores = []

    def store(source, target, semaphore):
        copy = pltpu.make_async_copy(source, target, semaphore)
        copy.start()
        stores.append(copy)

    stream[...] = jnp.zeros_like(stream)
    shifted[...] = jnp.zeros_like(shifted)
    for ref in (taps, mixed):
        ref[:pad, :] = jnp.zeros((pad, ref.shape[1]), ref.dtype)
        ref[pad + count :, :] = jnp.zeros((pad, ref.shape[1]), ref.dtype)

    piece_rows = pieces[0].shape[0] // (2 * grid_rows)
    tile = tile_rows * tile_cols
    for step_col in range(grid_cols):
        source_col = lax.bitwise_xor(col, step_col)
        for step_row in range(grid_rows):
            source_row = lax.rem(row + step_row, grid_rows)
            first = (step_col // 2 * grid_rows + step_row) * piece_rows
            piece = pieces[step_col % 2][first : first + piece_rows, :].astype(jnp.float32)
            back[
                pl.ds(pl.multiple_of(source_row * tile_rows, tile_rows), tile_rows),
                pl.ds(pl.multiple_of(source_col * tile_cols, tile_cols), tile_cols),
                :,
            ] = piece[:tile].reshape(tile_rows, tile_cols, channels)
            owner = source_row * grid_cols + source_col
            spread[pl.ds(pl.multiple_of(owner * 8, 8), 8), :] = piece[tile : tile + 8]
    owners = grid_rows * grid_cols
    for k in range(own):
        seq_lo[pl.ds(k, owners, stride=own), :] = spread[pl.ds(k, owners, stride=8), :]
        seq_hi[pl.ds(k, owners, stride=own), :] = spread[pl.ds(own + k, owners, stride=8), :]
    seq = jnp.concatenate([seq_lo[...], seq_hi[...]], axis=1).astype(jnp.bfloat16)

    def get(ref, part):
        return ref[part, :height, :].reshape(-1, channels)

    def put(ref, part, value):
        ref[part, :height, :] = value.reshape(CHUNK, height, channels)

    row_emb = dot(seq, embed[0], NN).astype(jnp.bfloat16).astype(jnp.float32)
    col_emb = dot(seq, embed[1], NN).astype(jnp.bfloat16).astype(jnp.float32)
    for part in chunks:
        stream[part, :height, :] = live[part, :height, :] * (
            row_emb[part, None, :] + col_emb[None, :height, :]
        )

    def lane_mean(x):
        return jnp.mean(x, axis=-1, keepdims=True)

    def flat(part):
        return slice(part.start * height, part.stop * height)

    row_mean = jnp.broadcast_to(lane_mean(row_emb), row_emb.shape)
    col_mean = jnp.broadcast_to(lane_mean(col_emb), col_emb.shape)
    for part in chunks:
        first = live[part, :height, :] * (row_mean[part, None, :] + col_mean[None, :height, :])
        guess[flat(part), :] = first.reshape(-1, channels)

    def moved(rows, by):
        return slice(pad + rows.start + by * height, pad + rows.stop + by * height)

    def store_shifted(part, value):
        shifted[part, margin : margin + height, :] = value.reshape(CHUNK, height, channels)

    def fill_taps(part, spacing):
        for b in (-1, 0, 1):
            start = margin + b * spacing
            value = shifted[part, start : start + height, :].reshape(-1, channels)
            taps[moved(flat(part), 0), (b + 1) * channels : (b + 2) * channels] = value.astype(
                jnp.bfloat16
            )

    def mix(part, matrix, dims):
        rows = moved(flat(part), 0)
        edge = 2 * channels
        low, high = (matrix[:edge], matrix[edge:])
        if dims is NT:
            low, high = (matrix[:, :edge], matrix[:, edge:])
        mixed[rows, :] = dot(taps[rows, :edge], low, dims) + dot(taps[rows, edge:], high, dims)

    def gather_rows(part, spacing):
        return sum(
            mixed[moved(flat(part), a * spacing), (a + 1) * channels : (a + 2) * channels]
            for a in (-1, 0, 1)
        )

    def block(layer, a, b):
        first = (3 * a + b) * channels
        return weights[layer, first : first + channels, :]

    for layer in range(LAYERS):
        spacing = 2**layer
        gain = gains[layer : layer + 1, :]
        for part in chunks:
            near = get(stream, part) - guess[flat(part), :]
            offset = lane_mean(near)
            variance = jnp.maximum(lane_mean(near * near) - offset * offset, 0.0)
            inv_std = lax.rsqrt(variance + eps)
            normalized = (near - offset) * inv_std
            scaled = normalized * gain
            decay = jnp.exp(jnp.minimum(scaled, 0.0))
            activated = jnp.maximum(scaled, 0.0) + (decay - 1.0)
            rows = flat(part)
            normed[layer, rows, :] = normalized
            inv[layer, rows, :] = jnp.broadcast_to(inv_std, normalized.shape)
            slope[layer, rows, :] = decay * get(live, part)
            store_shifted(part, activated)
            squashed[layer, rows, :] = activated.astype(jnp.bfloat16)
            fill_taps(part, spacing)
        wide = jnp.concatenate(
            [jnp.concatenate([block(layer, a, b) for b in range(3)], axis=0) for a in range(3)],
            axis=1,
        )
        for part in mix_parts(height):
            mix(part, wide, NN)
        for part in chunks:
            convolved = gather_rows(part, spacing)
            decay = jnp.exp(jnp.minimum(convolved, 0.0))
            rows = flat(part)
            conv_slope[layer, rows, :] = decay
            hidden = (jnp.maximum(convolved, 0.0) + (decay - 1.0)).astype(jnp.bfloat16)
            excited[layer, rows, :] = hidden
            both = jnp.concatenate([proj[layer], proj_mean[layer]], axis=1)
            update = dot(hidden, both, NN)
            alive = get(live, part)
            put(stream, part, get(stream, part) + alive * update[:, :channels])
            guess[rows, :] = guess[rows, :] + alive * update[:, channels:]

    pair_ref[...] = stream[
        pl.ds(pl.multiple_of(row * tile_rows, tile_rows), tile_rows),
        pl.ds(pl.multiple_of(col * tile_cols, tile_cols), tile_cols),
        :,
    ].astype(jnp.bfloat16)
    store(pair_ref, pair_hbm, sem.at[0])

    grad_scale = 1.0 / residues
    for part in chunks:
        put(back, part, get(back, part) * get(live, part))
    for layer in reversed(range(LAYERS)):
        spacing = 2**layer
        gain = gains[layer : layer + 1, :]
        for part in chunks:
            grad = get(back, part).astype(jnp.bfloat16)
            rows = flat(part)
            masked[rows, :] = grad
            store_shifted(part, dot(grad, proj[layer], NT) * conv_slope[layer, rows, :])
            fill_taps(part, -spacing)
        wide = jnp.concatenate(
            [jnp.concatenate([block(layer, a, b) for b in range(3)], axis=1) for a in range(3)],
            axis=0,
        )
        for part in mix_parts(height):
            mix(part, wide, NT)
        gain_total = jnp.zeros((1, channels), jnp.float32)
        for part in chunks:
            rows = flat(part)
            normalized = normed[layer, rows, :]
            d_scaled = gather_rows(part, -spacing) * slope[layer, rows, :]
            gain_total = gain_total + jnp.sum(d_scaled * normalized, axis=0, keepdims=True)
            d_norm = d_scaled * gain
            delta = inv[layer, rows, :] * (
                d_norm - lane_mean(d_norm) - normalized * lane_mean(d_norm * normalized)
            )
            put(back, part, get(back, part) + delta)
        gain_grad_ref[layer : layer + 1, :] = gain_total * grad_scale
        proj_grad_ref[layer] = dot(excited[layer], masked[...], TN) * grad_scale
        every = slice(0, count)
        for a in (-1, 0, 1):
            part_grad = dot(squashed[layer], taps[moved(every, -a * spacing), :], TN) * grad_scale
            for b in range(3):
                conv_grad[layer, 3 * (a + 1) + b] = part_grad[:, b * channels : (b + 1) * channels]
        store(conv_grad.at[layer], conv_grad_hbm.at[layer], grad_sem.at[0, layer])
        store(proj_grad_ref.at[layer], proj_grad_hbm.at[layer], grad_sem.at[1, layer])

    final = back[:height, :height, :]
    rest = jnp.zeros((residues - height, channels), jnp.float32)
    d_row = jnp.concatenate([jnp.sum(final, axis=1), rest], axis=0).astype(jnp.bfloat16)
    d_col = jnp.concatenate([jnp.sum(final, axis=0), rest], axis=0).astype(jnp.bfloat16)
    embed_grad_ref[0] = dot(seq, d_row, TN) * grad_scale
    embed_grad_ref[1] = dot(seq, d_col, TN) * grad_scale
    store(gain_grad_ref, gain_grad_hbm, sem.at[1])
    store(embed_grad_ref, embed_grad_hbm, sem.at[2])
    seq_grad = (dot(d_row, embed[0], NT) + dot(d_col, embed[1], NT)) / math.sqrt(residues)
    first = own * (row * grid_cols + col)
    for k in range(own):
        chosen = lax.broadcasted_iota(jnp.int32, seq_grad.shape, 0) == first + k
        seq_grad_ref[k : k + 1, :] = jnp.sum(
            jnp.where(chosen, seq_grad, 0.0), axis=0, keepdims=True
        )
    store(seq_grad_ref, seq_grad_hbm, sem.at[3])
    for copy in stores:
        copy.wait()


def replicated_body(
    seq_feat, lengths, embed_weight, norm_gain, conv_weight, proj_weight, pair_cotangent
):
    tile_rows, tile_cols, channels = pair_cotangent.shape
    grid_rows, grid_cols = lax.axis_size("row"), lax.axis_size("col")
    residues = tile_rows * grid_rows
    height = most_live(residues)
    margin = 2 ** (LAYERS - 1)
    own, features = seq_feat.shape
    f32, bf16 = jnp.float32, jnp.bfloat16
    vmem = pl.BlockSpec(memory_space=pltpu.VMEM)
    hbm = pl.BlockSpec(memory_space=pltpu.HBM)
    square = (residues, residues, channels)
    payload = pl.pallas_call(
        pack_kernel,
        out_shape=pltpu.VMEM((tile_rows * tile_cols + 8, channels), bf16),
    )(in_hbm(seq_feat), in_hbm(pair_cotangent))
    payload = lax.optimization_barrier(payload)
    def swap(x, axis, count, bit):
        return lax.ppermute(x, axis, [(i, i ^ bit) for i in range(count)])

    def rotate(x, axis, count, step):
        return lax.ppermute(x, axis, [(i, (i + step) % count) for i in range(count)])

    turns = [rotate(payload, "row", grid_rows, k) for k in reversed(range(1, grid_rows))]
    column = lax.optimization_barrier(jnp.concatenate([payload] + turns, axis=0))
    column, lengths = lax.optimization_barrier((column, lengths))
    held = (
        embed_weight,
        norm_gain,
        conv_weight.reshape(LAYERS, 9 * channels, channels),
        proj_weight,
    )
    live, *held = pl.pallas_call(
        setup_kernel,
        out_shape=[pltpu.VMEM(square, f32)]
        + [pltpu.VMEM(x.shape, x.dtype) for x in held + (proj_weight,)],
        in_specs=[hbm] * (1 + len(held)),
        scratch_shapes=[
            pltpu.SMEM(lengths.shape, jnp.int32),
            pltpu.SemaphoreType.DMA((1 + len(held),)),
        ],
        cost_estimate=pl.CostEstimate(flops=0, bytes_accessed=4 * 2**20, transcendentals=0),
    )(in_hbm(lengths), *[in_hbm(x) for x in held])

    chip = [column, swap(column, "col", grid_cols, 2)]
    chip, live, held = lax.optimization_barrier((chip, live, held))
    chip = lax.optimization_barrier(jnp.concatenate(chip, axis=0))
    pieces = [chip, swap(chip, "col", grid_cols, 1)]
    count = height * height
    edge = margin * height
    saved = (LAYERS, count, channels)
    results = (
        jax.ShapeDtypeStruct((tile_rows, tile_cols, channels), bf16),
        jax.ShapeDtypeStruct((own, features), f32),
        jax.ShapeDtypeStruct((2, features, channels), f32),
        jax.ShapeDtypeStruct((LAYERS, channels), f32),
        jax.ShapeDtypeStruct((LAYERS, 9, channels, channels), f32),
        jax.ShapeDtypeStruct((LAYERS, channels, channels), f32),
    )
    outs = pl.pallas_call(
        functools.partial(block_kernel, grid_rows, grid_cols),
        out_shape=results,
        in_specs=[vmem] * 8,
        out_specs=(hbm,) * len(results),
        scratch_shapes=[
            pltpu.VMEM(square, f32),
            pltpu.VMEM((count, channels), f32),
            pltpu.VMEM(square, f32),
            pltpu.VMEM((height, height + 2 * margin, channels), f32),
            pltpu.VMEM((count + 2 * edge, 3 * channels), bf16),
            pltpu.VMEM((count + 2 * edge, 3 * channels), f32),
            pltpu.VMEM(saved, f32),
            pltpu.VMEM(saved, f32),
            pltpu.VMEM(saved, f32),
            pltpu.VMEM(saved, bf16),
            pltpu.VMEM(saved, f32),
            pltpu.VMEM(saved, bf16),
            pltpu.VMEM((count, channels), bf16),
            pltpu.VMEM((8 * grid_rows * grid_cols, channels), f32),
            pltpu.VMEM((residues, channels), f32),
            pltpu.VMEM((residues, channels), f32),
            *[pltpu.VMEM(x.shape, x.dtype) for x in results],
            pltpu.SemaphoreType.DMA((4,)),
            pltpu.SemaphoreType.DMA((2, LAYERS)),
        ],
        compiler_params=pltpu.CompilerParams(vmem_limit_bytes=40 * 1024 * 1024),
    )(*pieces, live, *held)
    pair_output, seq_grad, embed_grad, gain_grad, conv_grad, proj_grad = outs
    return (
        pair_output,
        seq_grad,
        embed_grad,
        gain_grad,
        conv_grad.reshape(LAYERS, 3, 3, channels, channels),
        proj_grad,
    )


def body(seq_feat, lengths, embed_weight, norm_gain, conv_weight, proj_weight, pair_cotangent):
    residues = pair_cotangent.shape[0] * lax.axis_size("row")
    plan = replicated_body if residues <= 32 else tiled_body
    return plan(
        seq_feat, lengths, embed_weight, norm_gain, conv_weight, proj_weight, pair_cotangent
    )


def solution(mesh):
    placed = (
        P(("groups", "row", "col"), None),
        P("groups"),
        P(),
        P(),
        P(),
        P(),
        P(("groups", "row"), "col", None),
    )
    return jax.shard_map(
        body,
        mesh=mesh,
        in_specs=placed,
        out_specs=(
            P(("groups", "row"), "col", None),
            P(("groups", "row", "col"), None),
            P("groups", None, None),
            P("groups", None),
            P("groups", None, None, None, None),
            P("groups", None, None),
        ),
        check_vma=False,
    )
```

```python
import functools
import math

import jax
import jax.numpy as jnp
from jax import lax
from jax.experimental import pallas as pl
from jax.experimental.pallas import tpu as pltpu
from jax.sharding import PartitionSpec as P

LAYERS = 4


eps = 1e-05


def with_halo(x, sides, width):
    for axis, dim in sides:
        count, length = (lax.axis_size(axis), x.shape[dim])
        up = [(i, (i + 1) % count) for i in range(count - 1)]
        down = [(j, i) for i, j in up]
        last = lax.slice_in_dim(x, length - width, length, axis=dim)
        first = lax.slice_in_dim(x, 0, width, axis=dim)
        before = lax.ppermute(last, axis, up)
        after = lax.ppermute(first, axis, down)
        x = jnp.concatenate([before, x, after], axis=dim)
    return x


def elu_slope(values):
    return jnp.where(values > 0, 1.0, jnp.exp(jnp.minimum(values, 0.0)))


def normalize(stream, gain_row):
    average = jnp.mean(stream, axis=-1, keepdims=True)
    centred = stream - average
    variance = jnp.mean(centred * centred, axis=-1, keepdims=True)
    inv_std = lax.rsqrt(variance + eps)
    normalized = centred * inv_std
    return (normalized, inv_std, normalized * gain_row)


def conv_forward(padded, weight, spacing, height, width):
    channels = padded.shape[-1]
    summed = jnp.zeros((height * width, weight.shape[-1]), jnp.float32)
    for tap_row in range(3):
        for tap_col in range(3):
            window = padded[
                tap_row * spacing : tap_row * spacing + height,
                tap_col * spacing : tap_col * spacing + width,
                :,
            ]
            summed = summed + jnp.dot(
                window.reshape(height * width, channels),
                weight[tap_row, tap_col],
                preferred_element_type=jnp.float32,
            )
    return summed.reshape(height, width, -1)


def conv_backward(padded, weight, spacing, height, width):
    channels = padded.shape[-1]
    summed = jnp.zeros((height * width, weight.shape[-2]), jnp.float32)
    for tap_row in range(3):
        for tap_col in range(3):
            start_row = (2 - tap_row) * spacing
            start_col = (2 - tap_col) * spacing
            window = padded[start_row : start_row + height, start_col : start_col + width, :]
            summed = summed + jnp.dot(
                window.reshape(height * width, channels),
                weight[tap_row, tap_col].T,
                preferred_element_type=jnp.float32,
            )
    return summed.reshape(height, width, -1)


def conv_weight_grad(padded, grad_tile, spacing, height, width):
    channels = padded.shape[-1]
    flat_grad = grad_tile.reshape(height * width, -1)
    terms = []
    for tap_row in range(3):
        row_terms = []
        for tap_col in range(3):
            window = padded[
                tap_row * spacing : tap_row * spacing + height,
                tap_col * spacing : tap_col * spacing + width,
                :,
            ]
            row_terms.append(
                lax.dot_general(
                    window.reshape(height * width, channels),
                    flat_grad,
                    (((0,), (0,)), ((), ())),
                    preferred_element_type=jnp.float32,
                )
            )
        terms.append(jnp.stack(row_terms))
    return jnp.stack(terms)


def tiled_body(seq_feat, lengths, embed_weight, norm_gain, conv_weight, proj_weight, pair_cotangent):
    tile_rows = pair_cotangent.shape[0]
    tile_cols = pair_cotangent.shape[1]
    channels = pair_cotangent.shape[2]
    residues = tile_rows * lax.axis_size("row")
    row_start = lax.axis_index("row") * tile_rows
    col_start = lax.axis_index("col") * tile_cols
    row_live = (row_start + jnp.arange(tile_rows, dtype=jnp.int32) < lengths[0]).astype(jnp.float32)
    col_live = (col_start + jnp.arange(tile_cols, dtype=jnp.int32) < lengths[0]).astype(jnp.float32)
    live_mask = row_live[:, None, None] * col_live[None, :, None]
    gathered = lax.all_gather(seq_feat, ("row", "col"), axis=0, tiled=True)
    row_part = lax.dynamic_slice_in_dim(gathered, row_start, tile_rows, 0)
    col_part = lax.dynamic_slice_in_dim(gathered, col_start, tile_cols, 0)
    row_emb = jnp.dot(row_part, embed_weight[0], preferred_element_type=jnp.float32).astype(
        jnp.bfloat16
    )
    col_emb = jnp.dot(col_part, embed_weight[1], preferred_element_type=jnp.float32).astype(
        jnp.bfloat16
    )
    stream = live_mask * (
        row_emb.astype(jnp.float32)[:, None, :] + col_emb.astype(jnp.float32)[None, :, :]
    )
    stored = []
    for layer_number in range(LAYERS):
        spacing = 2**layer_number
        normalized, inv_std, scaled = normalize(stream, norm_gain[layer_number])
        squashed = (live_mask * jax.nn.elu(scaled)).astype(jnp.bfloat16)
        padded = with_halo(squashed, (("row", 0), ("col", 1)), spacing)
        convolved = conv_forward(padded, conv_weight[layer_number], spacing, tile_rows, tile_cols)
        excited = jax.nn.elu(convolved).astype(jnp.bfloat16)
        update = jnp.dot(
            excited.reshape(-1, channels),
            proj_weight[layer_number],
            preferred_element_type=jnp.float32,
        ).reshape(tile_rows, tile_cols, channels)
        stored.append((stream, padded, convolved, excited))
        stream = stream + live_mask * update
    pair_output = stream.astype(jnp.bfloat16)
    grad_scale = 1.0 / residues
    back_grad = pair_cotangent.astype(jnp.float32)
    gain_terms = [None] * LAYERS
    conv_terms = [None] * LAYERS
    proj_terms = [None] * LAYERS
    for layer_number in reversed(range(LAYERS)):
        spacing = 2**layer_number
        old_stream, padded, convolved, excited = stored[layer_number]
        masked = (live_mask * back_grad).astype(jnp.bfloat16)
        flat_masked = masked.reshape(-1, channels)
        proj_term = (
            lax.dot_general(
                excited.reshape(-1, channels),
                flat_masked,
                (((0,), (0,)), ((), ())),
                preferred_element_type=jnp.float32,
            )
            * grad_scale
        )
        d_excited = jnp.dot(
            flat_masked, proj_weight[layer_number].T, preferred_element_type=jnp.float32
        ).reshape(tile_rows, tile_cols, channels)
        d_pre = (d_excited * elu_slope(convolved)).astype(jnp.bfloat16)
        conv_term = conv_weight_grad(padded, d_pre, spacing, tile_rows, tile_cols) * grad_scale
        d_padded = with_halo(d_pre, (("row", 0), ("col", 1)), spacing)
        d_squashed = conv_backward(
            d_padded, conv_weight[layer_number], spacing, tile_rows, tile_cols
        )
        normalized, inv_std, scaled = normalize(old_stream, norm_gain[layer_number])
        d_scaled = live_mask * d_squashed * elu_slope(scaled)
        gain_term = jnp.sum(d_scaled * normalized, axis=(0, 1)) * grad_scale
        d_norm = d_scaled * norm_gain[layer_number]
        back_grad = back_grad + inv_std * (
            d_norm
            - jnp.mean(d_norm, axis=-1, keepdims=True)
            - normalized * jnp.mean(d_norm * normalized, axis=-1, keepdims=True)
        )
        gain_terms[layer_number] = gain_term
        conv_terms[layer_number] = conv_term
        proj_terms[layer_number] = proj_term
    final_masked = live_mask * back_grad
    row_totals = jnp.sum(final_masked, axis=1)
    col_totals = jnp.sum(final_masked, axis=0)
    d_row = lax.psum_scatter(row_totals, "col", scatter_dimension=0, tiled=True).astype(
        jnp.bfloat16
    )
    spread_cols = lax.dynamic_update_slice_in_dim(
        jnp.zeros((residues, channels), jnp.float32), col_totals, col_start, 0
    )
    d_col = lax.psum_scatter(spread_cols, ("row", "col"), scatter_dimension=0, tiled=True).astype(
        jnp.bfloat16
    )
    seq_grad = (
        jnp.dot(d_row, embed_weight[0].T, preferred_element_type=jnp.float32)
        + jnp.dot(d_col, embed_weight[1].T, preferred_element_type=jnp.float32)
    ) / math.sqrt(residues)
    embed_term = (
        jnp.stack(
            [
                lax.dot_general(
                    seq_feat, d_row, (((0,), (0,)), ((), ())), preferred_element_type=jnp.float32
                ),
                lax.dot_general(
                    seq_feat, d_col, (((0,), (0,)), ((), ())), preferred_element_type=jnp.float32
                ),
            ]
        )
        * grad_scale
    )
    gain_grad = jnp.stack(gain_terms)
    conv_grad = jnp.stack(conv_terms)
    proj_grad = jnp.stack(proj_terms)
    gain_grad, conv_grad, proj_grad, embed_grad = lax.psum(
        (gain_grad, conv_grad, proj_grad, embed_term), ("row", "col")
    )
    return (pair_output, seq_grad, embed_grad, gain_grad, conv_grad, proj_grad)


NT = (((1,), (1,)), ((), ()))
TN = (((0,), (0,)), ((), ()))
NN = (((1,), (0,)), ((), ()))


def dot(a, b, dims):
    return lax.dot_general(a, b, dims, preferred_element_type=jnp.float32)


def most_live(residues):
    return residues - residues // 4


CHUNK = 8


def mix_parts(height):
    return [slice(0, height)]


def ring_order(size):
    return list(range(0, size, 2)) + list(range(1, size, 2))


def ring_place(member, size):
    half, odd = (size + 1) // 2, lax.rem(member, 2)
    return lax.div(member, 2) + half * odd


def ring_member(place, size):
    half = (size + 1) // 2
    return jnp.where(place < half, 2 * place, 2 * (place - half) + 1)


def turn_order(size):
    return list(range(2, size)) + [1]


def in_hbm(x):
    return pltpu.with_memory_space_constraint(x, pltpu.HBM)


def pack_kernel(seq_ref, tile_ref, out_ref):
    rows, channels = out_ref.shape
    tile = tile_ref.shape[0] * tile_ref.shape[1]
    out_ref[:tile, :] = tile_ref[...].reshape(tile, channels)
    seq = seq_ref[...].astype(jnp.float32)
    own, features = seq.shape
    parts = [seq[:, k : k + channels] for k in range(0, features, channels)]
    parts.append(jnp.zeros((rows - tile - own * len(parts), channels), jnp.float32))
    out_ref[tile:, :] = jnp.concatenate(parts, axis=0).astype(out_ref.dtype)


def setup_kernel(*refs):
    lengths_hbm, refs = refs[0], refs[1:]
    half = (len(refs) - 4) // 2
    live_ref, mean_ref, lengths, sem = refs[half], refs[-3], refs[-2], refs[-1]
    copies = [
        pltpu.make_async_copy(refs[k], refs[half + 1 + k], sem.at[k]) for k in range(half)
    ]
    count_copy = pltpu.make_async_copy(lengths_hbm, lengths, sem.at[half])
    for copy in [count_copy] + copies:
        copy.start()
    pixel = jnp.maximum(
        lax.broadcasted_iota(jnp.int32, live_ref.shape, 0),
        lax.broadcasted_iota(jnp.int32, live_ref.shape, 1),
    )
    count_copy.wait()
    live_ref[...] = (pixel < lengths[0]).astype(live_ref.dtype)
    for copy in copies:
        copy.wait()
    proj = refs[2 * half][...].astype(jnp.float32)
    mean = jnp.mean(proj, axis=-1, keepdims=True)
    mean_ref[...] = jnp.broadcast_to(mean, proj.shape).astype(mean_ref.dtype)


def block_kernel(grid_rows, grid_cols, *refs):
    pieces, refs = refs[:2], refs[2:]
    live, embed, gains, weights, proj, proj_mean = refs[:6]
    (pair_hbm, seq_grad_hbm, embed_grad_hbm, gain_grad_hbm, conv_grad_hbm, proj_grad_hbm) = refs[6:12]
    (
        stream,
        guess,
        back,
        shifted,
        taps,
        mixed,
        normed,
        inv,
        slope,
        squashed,
        conv_slope,
        excited,
        masked,
        spread,
        seq_lo,
        seq_hi,
        pair_ref,
        seq_grad_ref,
        embed_grad_ref,
        gain_grad_ref,
        conv_grad,
        proj_grad_ref,
        sem,
        grad_sem,
    ) = refs[12:]
    tile_rows, tile_cols, channels = pair_ref.shape
    residues = tile_rows * grid_rows
    own = seq_grad_ref.shape[0]
    height = most_live(residues)
    count = height * height
    margin = 2 ** (LAYERS - 1)
    pad = margin * height
    chunks = [slice(k * CHUNK, (k + 1) * CHUNK) for k in range(height // CHUNK)]
    row, col = lax.axis_index("row"), lax.axis_index("col")
    stores = []

    def store(source, target, semaphore):
        copy = pltpu.make_async_copy(source, target, semaphore)
        copy.start()
        stores.append(copy)

    stream[...] = jnp.zeros_like(stream)
    shifted[...] = jnp.zeros_like(shifted)
    for ref in (taps, mixed):
        ref[:pad, :] = jnp.zeros((pad, ref.shape[1]), ref.dtype)
        ref[pad + count :, :] = jnp.zeros((pad, ref.shape[1]), ref.dtype)

    piece_rows = pieces[0].shape[0] // (2 * grid_rows)
    tile = tile_rows * tile_cols
    turns = [0] + turn_order(grid_rows)
    for step_col in range(grid_cols):
        source_col = lax.bitwise_xor(col, step_col)
        for step_row in range(grid_rows):
            place = lax.rem(ring_place(row, grid_rows) + grid_rows - turns[step_row], grid_rows)
            source_row = ring_member(place, grid_rows)
            first = (step_col // 2 * grid_rows + step_row) * piece_rows
            piece = pieces[step_col % 2][first : first + piece_rows, :].astype(jnp.float32)
            back[
                pl.ds(pl.multiple_of(source_row * tile_rows, tile_rows), tile_rows),
                pl.ds(pl.multiple_of(source_col * tile_cols, tile_cols), tile_cols),
                :,
            ] = piece[:tile].reshape(tile_rows, tile_cols, channels)
            owner = source_row * grid_cols + source_col
            spread[pl.ds(pl.multiple_of(owner * 8, 8), 8), :] = piece[tile : tile + 8]
    owners = grid_rows * grid_cols
    for k in range(own):
        seq_lo[pl.ds(k, owners, stride=own), :] = spread[pl.ds(k, owners, stride=8), :]
        seq_hi[pl.ds(k, owners, stride=own), :] = spread[pl.ds(own + k, owners, stride=8), :]
    seq = jnp.concatenate([seq_lo[...], seq_hi[...]], axis=1).astype(jnp.bfloat16)

    def get(ref, part):
        return ref[part, :height, :].reshape(-1, channels)

    def put(ref, part, value):
        ref[part, :height, :] = value.reshape(CHUNK, height, channels)

    row_emb = dot(seq, embed[0], NN).astype(jnp.bfloat16).astype(jnp.float32)
    col_emb = dot(seq, embed[1], NN).astype(jnp.bfloat16).astype(jnp.float32)
    for part in chunks:
        stream[part, :height, :] = live[part, :height, :] * (
            row_emb[part, None, :] + col_emb[None, :height, :]
        )

    def lane_mean(x):
        return jnp.mean(x, axis=-1, keepdims=True)

    def flat(part):
        return slice(part.start * height, part.stop * height)

    row_mean = jnp.broadcast_to(lane_mean(row_emb), row_emb.shape)
    col_mean = jnp.broadcast_to(lane_mean(col_emb), col_emb.shape)
    for part in chunks:
        first = live[part, :height, :] * (row_mean[part, None, :] + col_mean[None, :height, :])
        guess[flat(part), :] = first.reshape(-1, channels)

    def moved(rows, by):
        return slice(pad + rows.start + by * height, pad + rows.stop + by * height)

    def store_shifted(part, value):
        shifted[part, margin : margin + height, :] = value.reshape(CHUNK, height, channels)

    def fill_taps(part, spacing):
        for b in (-1, 0, 1):
            start = margin + b * spacing
            value = shifted[part, start : start + height, :].reshape(-1, channels)
            taps[moved(flat(part), 0), (b + 1) * channels : (b + 2) * channels] = value.astype(
                jnp.bfloat16
            )

    def mix(part, matrix, dims):
        rows = moved(flat(part), 0)
        edge = 2 * channels
        low, high = (matrix[:edge], matrix[edge:])
        if dims is NT:
            low, high = (matrix[:, :edge], matrix[:, edge:])
        mixed[rows, :] = dot(taps[rows, :edge], low, dims) + dot(taps[rows, edge:], high, dims)

    def gather_rows(part, spacing):
        return sum(
            mixed[moved(flat(part), a * spacing), (a + 1) * channels : (a + 2) * channels]
            for a in (-1, 0, 1)
        )

    def block(layer, a, b):
        first = (3 * a + b) * channels
        return weights[layer, first : first + channels, :]

    for layer in range(LAYERS):
        spacing = 2**layer
        gain = gains[layer : layer + 1, :]
        for part in chunks:
            near = get(stream, part) - guess[flat(part), :]
            offset = lane_mean(near)
            variance = jnp.maximum(lane_mean(near * near) - offset * offset, 0.0)
            inv_std = lax.rsqrt(variance + eps)
            normalized = (near - offset) * inv_std
            scaled = normalized * gain
            decay = jnp.exp(jnp.minimum(scaled, 0.0))
            activated = jnp.maximum(scaled, 0.0) + (decay - 1.0)
            rows = flat(part)
            normed[layer, rows, :] = normalized
            inv[layer, rows, :] = jnp.broadcast_to(inv_std, normalized.shape)
            slope[layer, rows, :] = decay * get(live, part)
            store_shifted(part, activated)
            squashed[layer, rows, :] = activated.astype(jnp.bfloat16)
            fill_taps(part, spacing)
        wide = jnp.concatenate(
            [jnp.concatenate([block(layer, a, b) for b in range(3)], axis=0) for a in range(3)],
            axis=1,
        )
        for part in mix_parts(height):
            mix(part, wide, NN)
        for part in chunks:
            convolved = gather_rows(part, spacing)
            decay = jnp.exp(jnp.minimum(convolved, 0.0))
            rows = flat(part)
            conv_slope[layer, rows, :] = decay
            hidden = (jnp.maximum(convolved, 0.0) + (decay - 1.0)).astype(jnp.bfloat16)
            excited[layer, rows, :] = hidden
            both = jnp.concatenate([proj[layer], proj_mean[layer]], axis=1)
            update = dot(hidden, both, NN)
            alive = get(live, part)
            put(stream, part, get(stream, part) + alive * update[:, :channels])
            guess[rows, :] = guess[rows, :] + alive * update[:, channels:]

    pair_ref[...] = stream[
        pl.ds(pl.multiple_of(row * tile_rows, tile_rows), tile_rows),
        pl.ds(pl.multiple_of(col * tile_cols, tile_cols), tile_cols),
        :,
    ].astype(jnp.bfloat16)
    store(pair_ref, pair_hbm, sem.at[0])

    grad_scale = 1.0 / residues
    for part in chunks:
        put(back, part, get(back, part) * get(live, part))
    for layer in reversed(range(LAYERS)):
        spacing = 2**layer
        gain = gains[layer : layer + 1, :]
        for part in chunks:
            grad = get(back, part).astype(jnp.bfloat16)
            rows = flat(part)
            masked[rows, :] = grad
            store_shifted(part, dot(grad, proj[layer], NT) * conv_slope[layer, rows, :])
            fill_taps(part, -spacing)
        wide = jnp.concatenate(
            [jnp.concatenate([block(layer, a, b) for b in range(3)], axis=1) for a in range(3)],
            axis=0,
        )
        for part in mix_parts(height):
            mix(part, wide, NT)
        gain_total = jnp.zeros((1, channels), jnp.float32)
        for part in chunks:
            rows = flat(part)
            normalized = normed[layer, rows, :]
            d_scaled = gather_rows(part, -spacing) * slope[layer, rows, :]
            gain_total = gain_total + jnp.sum(d_scaled * normalized, axis=0, keepdims=True)
            d_norm = d_scaled * gain
            delta = inv[layer, rows, :] * (
                d_norm - lane_mean(d_norm) - normalized * lane_mean(d_norm * normalized)
            )
            put(back, part, get(back, part) + delta)
        gain_grad_ref[layer : layer + 1, :] = gain_total * grad_scale
        proj_grad_ref[layer] = dot(excited[layer], masked[...], TN) * grad_scale
        every = slice(0, count)
        for a in (-1, 0, 1):
            part_grad = dot(squashed[layer], taps[moved(every, -a * spacing), :], TN) * grad_scale
            for b in range(3):
                conv_grad[layer, 3 * (a + 1) + b] = part_grad[:, b * channels : (b + 1) * channels]
        store(conv_grad.at[layer], conv_grad_hbm.at[layer], grad_sem.at[0, layer])
        store(proj_grad_ref.at[layer], proj_grad_hbm.at[layer], grad_sem.at[1, layer])

    final = back[:height, :height, :]
    rest = jnp.zeros((residues - height, channels), jnp.float32)
    d_row = jnp.concatenate([jnp.sum(final, axis=1), rest], axis=0).astype(jnp.bfloat16)
    d_col = jnp.concatenate([jnp.sum(final, axis=0), rest], axis=0).astype(jnp.bfloat16)
    embed_grad_ref[0] = dot(seq, d_row, TN) * grad_scale
    embed_grad_ref[1] = dot(seq, d_col, TN) * grad_scale
    store(gain_grad_ref, gain_grad_hbm, sem.at[1])
    store(embed_grad_ref, embed_grad_hbm, sem.at[2])
    seq_grad = (dot(d_row, embed[0], NT) + dot(d_col, embed[1], NT)) / math.sqrt(residues)
    first = own * (row * grid_cols + col)
    for k in range(own):
        chosen = lax.broadcasted_iota(jnp.int32, seq_grad.shape, 0) == first + k
        seq_grad_ref[k : k + 1, :] = jnp.sum(
            jnp.where(chosen, seq_grad, 0.0), axis=0, keepdims=True
        )
    store(seq_grad_ref, seq_grad_hbm, sem.at[3])
    for copy in stores:
        copy.wait()


def replicated_body(
    seq_feat, lengths, embed_weight, norm_gain, conv_weight, proj_weight, pair_cotangent
):
    tile_rows, tile_cols, channels = pair_cotangent.shape
    grid_rows, grid_cols = lax.axis_size("row"), lax.axis_size("col")
    residues = tile_rows * grid_rows
    height = most_live(residues)
    margin = 2 ** (LAYERS - 1)
    own, features = seq_feat.shape
    f32, bf16 = jnp.float32, jnp.bfloat16
    vmem = pl.BlockSpec(memory_space=pltpu.VMEM)
    hbm = pl.BlockSpec(memory_space=pltpu.HBM)
    square = (residues, residues, channels)
    payload = pl.pallas_call(
        pack_kernel,
        out_shape=pltpu.VMEM((tile_rows * tile_cols + 8, channels), bf16),
    )(in_hbm(seq_feat), in_hbm(pair_cotangent))
    payload = lax.optimization_barrier(payload)
    def swap(x, axis, count, bit):
        return lax.ppermute(x, axis, [(i, i ^ bit) for i in range(count)])

    ring = ring_order(grid_rows)
    turns = [
        lax.ppermute(
            payload,
            "row",
            [(ring[i], ring[(i + k) % grid_rows]) for i in range(grid_rows)],
        )
        for k in turn_order(grid_rows)
    ]
    column = lax.optimization_barrier(jnp.concatenate([payload] + turns, axis=0))
    column, lengths = lax.optimization_barrier((column, lengths))
    held = (
        embed_weight,
        norm_gain,
        conv_weight.reshape(LAYERS, 9 * channels, channels),
        proj_weight,
    )
    live, *held = pl.pallas_call(
        setup_kernel,
        out_shape=[pltpu.VMEM(square, f32)]
        + [pltpu.VMEM(x.shape, x.dtype) for x in held + (proj_weight,)],
        in_specs=[hbm] * (1 + len(held)),
        scratch_shapes=[
            pltpu.SMEM(lengths.shape, jnp.int32),
            pltpu.SemaphoreType.DMA((1 + len(held),)),
        ],
        cost_estimate=pl.CostEstimate(flops=0, bytes_accessed=4 * 2**20, transcendentals=0),
    )(in_hbm(lengths), *[in_hbm(x) for x in held])

    chip = [column, swap(column, "col", grid_cols, 2)]
    chip, live, held = lax.optimization_barrier((chip, live, held))
    chip = lax.optimization_barrier(jnp.concatenate(chip, axis=0))
    pieces = [chip, swap(chip, "col", grid_cols, 1)]
    count = height * height
    edge = margin * height
    saved = (LAYERS, count, channels)
    results = (
        jax.ShapeDtypeStruct((tile_rows, tile_cols, channels), bf16),
        jax.ShapeDtypeStruct((own, features), f32),
        jax.ShapeDtypeStruct((2, features, channels), f32),
        jax.ShapeDtypeStruct((LAYERS, channels), f32),
        jax.ShapeDtypeStruct((LAYERS, 9, channels, channels), f32),
        jax.ShapeDtypeStruct((LAYERS, channels, channels), f32),
    )
    outs = pl.pallas_call(
        functools.partial(block_kernel, grid_rows, grid_cols),
        out_shape=results,
        in_specs=[vmem] * 8,
        out_specs=(hbm,) * len(results),
        scratch_shapes=[
            pltpu.VMEM(square, f32),
            pltpu.VMEM((count, channels), f32),
            pltpu.VMEM(square, f32),
            pltpu.VMEM((height, height + 2 * margin, channels), f32),
            pltpu.VMEM((count + 2 * edge, 3 * channels), bf16),
            pltpu.VMEM((count + 2 * edge, 3 * channels), f32),
            pltpu.VMEM(saved, f32),
            pltpu.VMEM(saved, f32),
            pltpu.VMEM(saved, f32),
            pltpu.VMEM(saved, bf16),
            pltpu.VMEM(saved, f32),
            pltpu.VMEM(saved, bf16),
            pltpu.VMEM((count, channels), bf16),
            pltpu.VMEM((8 * grid_rows * grid_cols, channels), f32),
            pltpu.VMEM((residues, channels), f32),
            pltpu.VMEM((residues, channels), f32),
            *[pltpu.VMEM(x.shape, x.dtype) for x in results],
            pltpu.SemaphoreType.DMA((4,)),
            pltpu.SemaphoreType.DMA((2, LAYERS)),
        ],
        compiler_params=pltpu.CompilerParams(vmem_limit_bytes=40 * 1024 * 1024),
    )(*pieces, live, *held)
    pair_output, seq_grad, embed_grad, gain_grad, conv_grad, proj_grad = outs
    return (
        pair_output,
        seq_grad,
        embed_grad,
        gain_grad,
        conv_grad.reshape(LAYERS, 3, 3, channels, channels),
        proj_grad,
    )


def map_fits(grid_cols, tile_rows, residues, channels):
    height = most_live(residues)
    held = height * height * channels * LAYERS * 24
    return grid_cols == 4 and tile_rows % 8 == 0 and height % CHUNK == 0 and held <= 16 * 2**20


def body(seq_feat, lengths, embed_weight, norm_gain, conv_weight, proj_weight, pair_cotangent):
    tile_rows, _, channels = pair_cotangent.shape
    residues = tile_rows * lax.axis_size("row")
    whole = map_fits(lax.axis_size("col"), tile_rows, residues, channels)
    plan = replicated_body if whole else tiled_body
    return plan(
        seq_feat, lengths, embed_weight, norm_gain, conv_weight, proj_weight, pair_cotangent
    )


def solution(mesh):
    placed = (
        P(("groups", "row", "col"), None),
        P("groups"),
        P(),
        P(),
        P(),
        P(),
        P(("groups", "row"), "col", None),
    )
    return jax.shard_map(
        body,
        mesh=mesh,
        in_specs=placed,
        out_specs=(
            P(("groups", "row"), "col", None),
            P(("groups", "row", "col"), None),
            P("groups", None, None),
            P("groups", None),
            P("groups", None, None, None, None),
            P("groups", None, None),
        ),
        check_vma=False,
    )
```

```python
import functools
import math

import jax
import jax.numpy as jnp
from jax import lax
from jax.experimental import pallas as pl
from jax.experimental.pallas import tpu as pltpu
from jax.sharding import PartitionSpec as P

LAYERS = 4


eps = 1e-05


def with_halo(x, sides, width):
    for axis, dim in sides:
        count, length = (lax.axis_size(axis), x.shape[dim])
        up = [(i, (i + 1) % count) for i in range(count - 1)]
        down = [(j, i) for i, j in up]
        last = lax.slice_in_dim(x, length - width, length, axis=dim)
        first = lax.slice_in_dim(x, 0, width, axis=dim)
        before = lax.ppermute(last, axis, up)
        after = lax.ppermute(first, axis, down)
        x = jnp.concatenate([before, x, after], axis=dim)
    return x


def elu_slope(values):
    return jnp.where(values > 0, 1.0, jnp.exp(jnp.minimum(values, 0.0)))


def normalize(stream, gain_row):
    average = jnp.mean(stream, axis=-1, keepdims=True)
    centred = stream - average
    variance = jnp.mean(centred * centred, axis=-1, keepdims=True)
    inv_std = lax.rsqrt(variance + eps)
    normalized = centred * inv_std
    return (normalized, inv_std, normalized * gain_row)


def conv_forward(padded, weight, spacing, height, width):
    channels = padded.shape[-1]
    summed = jnp.zeros((height * width, weight.shape[-1]), jnp.float32)
    for tap_row in range(3):
        for tap_col in range(3):
            window = padded[
                tap_row * spacing : tap_row * spacing + height,
                tap_col * spacing : tap_col * spacing + width,
                :,
            ]
            summed = summed + jnp.dot(
                window.reshape(height * width, channels),
                weight[tap_row, tap_col],
                preferred_element_type=jnp.float32,
            )
    return summed.reshape(height, width, -1)


def conv_backward(padded, weight, spacing, height, width):
    channels = padded.shape[-1]
    summed = jnp.zeros((height * width, weight.shape[-2]), jnp.float32)
    for tap_row in range(3):
        for tap_col in range(3):
            start_row = (2 - tap_row) * spacing
            start_col = (2 - tap_col) * spacing
            window = padded[start_row : start_row + height, start_col : start_col + width, :]
            summed = summed + jnp.dot(
                window.reshape(height * width, channels),
                weight[tap_row, tap_col].T,
                preferred_element_type=jnp.float32,
            )
    return summed.reshape(height, width, -1)


def conv_weight_grad(padded, grad_tile, spacing, height, width):
    channels = padded.shape[-1]
    flat_grad = grad_tile.reshape(height * width, -1)
    terms = []
    for tap_row in range(3):
        row_terms = []
        for tap_col in range(3):
            window = padded[
                tap_row * spacing : tap_row * spacing + height,
                tap_col * spacing : tap_col * spacing + width,
                :,
            ]
            row_terms.append(
                lax.dot_general(
                    window.reshape(height * width, channels),
                    flat_grad,
                    (((0,), (0,)), ((), ())),
                    preferred_element_type=jnp.float32,
                )
            )
        terms.append(jnp.stack(row_terms))
    return jnp.stack(terms)


def tiled_body(seq_feat, lengths, embed_weight, norm_gain, conv_weight, proj_weight, pair_cotangent):
    tile_rows = pair_cotangent.shape[0]
    tile_cols = pair_cotangent.shape[1]
    channels = pair_cotangent.shape[2]
    residues = tile_rows * lax.axis_size("row")
    row_start = lax.axis_index("row") * tile_rows
    col_start = lax.axis_index("col") * tile_cols
    row_live = (row_start + jnp.arange(tile_rows, dtype=jnp.int32) < lengths[0]).astype(jnp.float32)
    col_live = (col_start + jnp.arange(tile_cols, dtype=jnp.int32) < lengths[0]).astype(jnp.float32)
    live_mask = row_live[:, None, None] * col_live[None, :, None]
    gathered = lax.all_gather(seq_feat, ("row", "col"), axis=0, tiled=True)
    row_part = lax.dynamic_slice_in_dim(gathered, row_start, tile_rows, 0)
    col_part = lax.dynamic_slice_in_dim(gathered, col_start, tile_cols, 0)
    row_emb = jnp.dot(row_part, embed_weight[0], preferred_element_type=jnp.float32).astype(
        jnp.bfloat16
    )
    col_emb = jnp.dot(col_part, embed_weight[1], preferred_element_type=jnp.float32).astype(
        jnp.bfloat16
    )
    stream = live_mask * (
        row_emb.astype(jnp.float32)[:, None, :] + col_emb.astype(jnp.float32)[None, :, :]
    )
    stored = []
    for layer_number in range(LAYERS):
        spacing = 2**layer_number
        normalized, inv_std, scaled = normalize(stream, norm_gain[layer_number])
        squashed = (live_mask * jax.nn.elu(scaled)).astype(jnp.bfloat16)
        padded = with_halo(squashed, (("row", 0), ("col", 1)), spacing)
        convolved = conv_forward(padded, conv_weight[layer_number], spacing, tile_rows, tile_cols)
        excited = jax.nn.elu(convolved).astype(jnp.bfloat16)
        update = jnp.dot(
            excited.reshape(-1, channels),
            proj_weight[layer_number],
            preferred_element_type=jnp.float32,
        ).reshape(tile_rows, tile_cols, channels)
        stored.append((stream, padded, convolved, excited))
        stream = stream + live_mask * update
    pair_output = stream.astype(jnp.bfloat16)
    grad_scale = 1.0 / residues
    back_grad = pair_cotangent.astype(jnp.float32)
    gain_terms = [None] * LAYERS
    conv_terms = [None] * LAYERS
    proj_terms = [None] * LAYERS
    for layer_number in reversed(range(LAYERS)):
        spacing = 2**layer_number
        old_stream, padded, convolved, excited = stored[layer_number]
        masked = (live_mask * back_grad).astype(jnp.bfloat16)
        flat_masked = masked.reshape(-1, channels)
        proj_term = (
            lax.dot_general(
                excited.reshape(-1, channels),
                flat_masked,
                (((0,), (0,)), ((), ())),
                preferred_element_type=jnp.float32,
            )
            * grad_scale
        )
        d_excited = jnp.dot(
            flat_masked, proj_weight[layer_number].T, preferred_element_type=jnp.float32
        ).reshape(tile_rows, tile_cols, channels)
        d_pre = (d_excited * elu_slope(convolved)).astype(jnp.bfloat16)
        conv_term = conv_weight_grad(padded, d_pre, spacing, tile_rows, tile_cols) * grad_scale
        d_padded = with_halo(d_pre, (("row", 0), ("col", 1)), spacing)
        d_squashed = conv_backward(
            d_padded, conv_weight[layer_number], spacing, tile_rows, tile_cols
        )
        normalized, inv_std, scaled = normalize(old_stream, norm_gain[layer_number])
        d_scaled = live_mask * d_squashed * elu_slope(scaled)
        gain_term = jnp.sum(d_scaled * normalized, axis=(0, 1)) * grad_scale
        d_norm = d_scaled * norm_gain[layer_number]
        back_grad = back_grad + inv_std * (
            d_norm
            - jnp.mean(d_norm, axis=-1, keepdims=True)
            - normalized * jnp.mean(d_norm * normalized, axis=-1, keepdims=True)
        )
        gain_terms[layer_number] = gain_term
        conv_terms[layer_number] = conv_term
        proj_terms[layer_number] = proj_term
    final_masked = live_mask * back_grad
    row_totals = jnp.sum(final_masked, axis=1)
    col_totals = jnp.sum(final_masked, axis=0)
    d_row = lax.psum_scatter(row_totals, "col", scatter_dimension=0, tiled=True).astype(
        jnp.bfloat16
    )
    spread_cols = lax.dynamic_update_slice_in_dim(
        jnp.zeros((residues, channels), jnp.float32), col_totals, col_start, 0
    )
    d_col = lax.psum_scatter(spread_cols, ("row", "col"), scatter_dimension=0, tiled=True).astype(
        jnp.bfloat16
    )
    seq_grad = (
        jnp.dot(d_row, embed_weight[0].T, preferred_element_type=jnp.float32)
        + jnp.dot(d_col, embed_weight[1].T, preferred_element_type=jnp.float32)
    ) / math.sqrt(residues)
    embed_term = (
        jnp.stack(
            [
                lax.dot_general(
                    seq_feat, d_row, (((0,), (0,)), ((), ())), preferred_element_type=jnp.float32
                ),
                lax.dot_general(
                    seq_feat, d_col, (((0,), (0,)), ((), ())), preferred_element_type=jnp.float32
                ),
            ]
        )
        * grad_scale
    )
    gain_grad = jnp.stack(gain_terms)
    conv_grad = jnp.stack(conv_terms)
    proj_grad = jnp.stack(proj_terms)
    gain_grad, conv_grad, proj_grad, embed_grad = lax.psum(
        (gain_grad, conv_grad, proj_grad, embed_term), ("row", "col")
    )
    return (pair_output, seq_grad, embed_grad, gain_grad, conv_grad, proj_grad)


NT = (((1,), (1,)), ((), ()))
TN = (((0,), (0,)), ((), ()))
NN = (((1,), (0,)), ((), ()))


def dot(a, b, dims):
    return lax.dot_general(a, b, dims, preferred_element_type=jnp.float32)


def most_live(residues):
    return residues - residues // 4


CHUNK = 24


def mix_parts(height):
    return [slice(0, height)]


def ring_order(size):
    return list(range(0, size, 2)) + list(range(1, size, 2))


def ring_place(member, size):
    half, odd = (size + 1) // 2, lax.rem(member, 2)
    return lax.div(member, 2) + half * odd


def ring_member(place, size):
    half = (size + 1) // 2
    return jnp.where(place < half, 2 * place, 2 * (place - half) + 1)


def turn_order(size):
    return list(range(2, size)) + [1]


def in_hbm(x):
    return pltpu.with_memory_space_constraint(x, pltpu.HBM)


def pack_kernel(seq_ref, tile_ref, out_ref):
    rows, channels = out_ref.shape
    tile = tile_ref.shape[0] * tile_ref.shape[1]
    out_ref[:tile, :] = tile_ref[...].reshape(tile, channels)
    seq = seq_ref[...].astype(jnp.float32)
    own, features = seq.shape
    parts = [seq[:, k : k + channels] for k in range(0, features, channels)]
    parts.append(jnp.zeros((rows - tile - own * len(parts), channels), jnp.float32))
    out_ref[tile:, :] = jnp.concatenate(parts, axis=0).astype(out_ref.dtype)


def setup_kernel(*refs):
    lengths_hbm, refs = refs[0], refs[1:]
    half = (len(refs) - 4) // 2
    live_ref, mean_ref, lengths, sem = refs[half], refs[-3], refs[-2], refs[-1]
    copies = [
        pltpu.make_async_copy(refs[k], refs[half + 1 + k], sem.at[k]) for k in range(half)
    ]
    count_copy = pltpu.make_async_copy(lengths_hbm, lengths, sem.at[half])
    for copy in [count_copy] + copies:
        copy.start()
    pixel = jnp.maximum(
        lax.broadcasted_iota(jnp.int32, live_ref.shape, 0),
        lax.broadcasted_iota(jnp.int32, live_ref.shape, 1),
    )
    count_copy.wait()
    live_ref[...] = (pixel < lengths[0]).astype(live_ref.dtype)
    for copy in copies:
        copy.wait()
    proj = refs[2 * half][...].astype(jnp.float32)
    mean = jnp.mean(proj, axis=-1, keepdims=True)
    mean_ref[...] = jnp.broadcast_to(mean, proj.shape).astype(mean_ref.dtype)


def block_kernel(grid_rows, grid_cols, *refs):
    pieces, refs = (refs[0], refs[2], refs[3], refs[1]), refs[4:]
    live, embed, gains, weights, proj, proj_mean = refs[:6]
    (pair_hbm, seq_grad_hbm, embed_grad_hbm, gain_grad_hbm, conv_grad_hbm, proj_grad_hbm) = refs[6:12]
    (
        stream,
        guess,
        back,
        shifted,
        taps,
        mixed,
        normed,
        inv,
        slope,
        squashed,
        conv_slope,
        excited,
        masked,
        spread,
        seq_lo,
        seq_hi,
        pair_ref,
        seq_grad_ref,
        embed_grad_ref,
        gain_grad_ref,
        conv_grad,
        proj_grad_ref,
        sem,
        grad_sem,
    ) = refs[12:]
    tile_rows, tile_cols, channels = pair_ref.shape
    residues = tile_rows * grid_rows
    own = seq_grad_ref.shape[0]
    height = most_live(residues)
    count = height * height
    margin = 2 ** (LAYERS - 1)
    pad = margin * height
    chunks = [slice(k * CHUNK, (k + 1) * CHUNK) for k in range(height // CHUNK)]
    row, col = lax.axis_index("row"), lax.axis_index("col")
    stores = []

    def store(source, target, semaphore):
        copy = pltpu.make_async_copy(source, target, semaphore)
        copy.start()
        stores.append(copy)

    dead = residues - height
    stream[height:, :, :] = jnp.zeros((dead, residues, channels), jnp.float32)
    stream[:height, height:, :] = jnp.zeros((height, dead, channels), jnp.float32)
    shifted[:, :margin, :] = jnp.zeros((height, margin, channels), jnp.float32)
    shifted[:, margin + height :, :] = jnp.zeros((height, margin, channels), jnp.float32)
    for ref in (taps, mixed):
        ref[:pad, :] = jnp.zeros((pad, ref.shape[1]), ref.dtype)
        ref[pad + count :, :] = jnp.zeros((pad, ref.shape[1]), ref.dtype)

    piece_rows = pieces[0].shape[0] // grid_rows
    tile = tile_rows * tile_cols
    turns = [0] + turn_order(grid_rows)
    for step_col in range(grid_cols):
        source_col = lax.bitwise_xor(col, step_col)
        for step_row in range(grid_rows):
            place = lax.rem(ring_place(row, grid_rows) + grid_rows - turns[step_row], grid_rows)
            source_row = ring_member(place, grid_rows)
            first = step_row * piece_rows
            piece = pieces[step_col][first : first + piece_rows, :].astype(jnp.float32)
            back[
                pl.ds(pl.multiple_of(source_row * tile_rows, tile_rows), tile_rows),
                pl.ds(pl.multiple_of(source_col * tile_cols, tile_cols), tile_cols),
                :,
            ] = piece[:tile].reshape(tile_rows, tile_cols, channels)
            owner = source_row * grid_cols + source_col
            spread[pl.ds(pl.multiple_of(owner * 8, 8), 8), :] = piece[tile : tile + 8]
    owners = grid_rows * grid_cols
    for k in range(own):
        seq_lo[pl.ds(k, owners, stride=own), :] = spread[pl.ds(k, owners, stride=8), :]
        seq_hi[pl.ds(k, owners, stride=own), :] = spread[pl.ds(own + k, owners, stride=8), :]
    seq = jnp.concatenate([seq_lo[...], seq_hi[...]], axis=1).astype(jnp.bfloat16)

    def get(ref, part):
        return ref[part, :height, :].reshape(-1, channels)

    def put(ref, part, value):
        ref[part, :height, :] = value.reshape(CHUNK, height, channels)

    row_emb = dot(seq, embed[0], NN).astype(jnp.bfloat16).astype(jnp.float32)
    col_emb = dot(seq, embed[1], NN).astype(jnp.bfloat16).astype(jnp.float32)
    for part in chunks:
        stream[part, :height, :] = live[part, :height, :] * (
            row_emb[part, None, :] + col_emb[None, :height, :]
        )

    def lane_mean(x):
        return jnp.mean(x, axis=-1, keepdims=True)

    def flat(part):
        return slice(part.start * height, part.stop * height)

    row_mean = jnp.broadcast_to(lane_mean(row_emb), row_emb.shape)
    col_mean = jnp.broadcast_to(lane_mean(col_emb), col_emb.shape)
    for part in chunks:
        first = live[part, :height, :] * (row_mean[part, None, :] + col_mean[None, :height, :])
        guess[flat(part), :] = first.reshape(-1, channels)

    def moved(rows, by):
        return slice(pad + rows.start + by * height, pad + rows.stop + by * height)

    def store_shifted(part, value):
        shifted[part, margin : margin + height, :] = value.reshape(CHUNK, height, channels)

    def fill_taps(part, spacing):
        for b in (-1, 0, 1):
            start = margin + b * spacing
            value = shifted[part, start : start + height, :].reshape(-1, channels)
            taps[moved(flat(part), 0), (b + 1) * channels : (b + 2) * channels] = value.astype(
                jnp.bfloat16
            )

    def mix(part, matrix, dims):
        rows = moved(flat(part), 0)
        edge = 2 * channels
        low, high = (matrix[:edge], matrix[edge:])
        if dims is NT:
            low, high = (matrix[:, :edge], matrix[:, edge:])
        mixed[rows, :] = dot(taps[rows, :edge], low, dims) + dot(taps[rows, edge:], high, dims)

    def gather_rows(part, spacing):
        return sum(
            mixed[moved(flat(part), a * spacing), (a + 1) * channels : (a + 2) * channels]
            for a in (-1, 0, 1)
        )

    def block(layer, a, b):
        first = (3 * a + b) * channels
        return weights[layer, first : first + channels, :]

    for layer in range(LAYERS):
        spacing = 2**layer
        gain = gains[layer : layer + 1, :]
        for part in chunks:
            near = get(stream, part) - guess[flat(part), :]
            offset = lane_mean(near)
            variance = jnp.maximum(lane_mean(near * near) - offset * offset, 0.0)
            inv_std = lax.rsqrt(variance + eps)
            normalized = (near - offset) * inv_std
            scaled = normalized * gain
            decay = jnp.exp(jnp.minimum(scaled, 0.0))
            activated = jnp.maximum(scaled, 0.0) + (decay - 1.0)
            rows = flat(part)
            normed[layer, rows, :] = normalized
            inv[layer, rows, :] = jnp.broadcast_to(inv_std, normalized.shape)
            slope[layer, rows, :] = decay * get(live, part)
            store_shifted(part, activated)
            squashed[layer, rows, :] = activated.astype(jnp.bfloat16)
            fill_taps(part, spacing)
        wide = jnp.concatenate(
            [jnp.concatenate([block(layer, a, b) for b in range(3)], axis=0) for a in range(3)],
            axis=1,
        )
        for part in mix_parts(height):
            mix(part, wide, NN)
        for part in chunks:
            convolved = gather_rows(part, spacing)
            decay = jnp.exp(jnp.minimum(convolved, 0.0))
            rows = flat(part)
            conv_slope[layer, rows, :] = decay
            hidden = (jnp.maximum(convolved, 0.0) + (decay - 1.0)).astype(jnp.bfloat16)
            excited[layer, rows, :] = hidden
            both = jnp.concatenate([proj[layer], proj_mean[layer]], axis=1)
            update = dot(hidden, both, NN)
            alive = get(live, part)
            put(stream, part, get(stream, part) + alive * update[:, :channels])
            guess[rows, :] = guess[rows, :] + alive * update[:, channels:]

    pair_ref[...] = stream[
        pl.ds(pl.multiple_of(row * tile_rows, tile_rows), tile_rows),
        pl.ds(pl.multiple_of(col * tile_cols, tile_cols), tile_cols),
        :,
    ].astype(jnp.bfloat16)
    store(pair_ref, pair_hbm, sem.at[0])

    grad_scale = 1.0 / residues
    for part in chunks:
        put(back, part, get(back, part) * get(live, part))
    for layer in reversed(range(LAYERS)):
        spacing = 2**layer
        gain = gains[layer : layer + 1, :]
        for part in chunks:
            grad = get(back, part).astype(jnp.bfloat16)
            rows = flat(part)
            masked[rows, :] = grad
            store_shifted(part, dot(grad, proj[layer], NT) * conv_slope[layer, rows, :])
            fill_taps(part, -spacing)
        wide = jnp.concatenate(
            [jnp.concatenate([block(layer, a, b) for b in range(3)], axis=1) for a in range(3)],
            axis=0,
        )
        for part in mix_parts(height):
            mix(part, wide, NT)
        proj_grad_ref[layer] = dot(excited[layer], masked[...], TN) * grad_scale
        every = slice(0, count)
        for a in (-1, 0, 1):
            part_grad = dot(squashed[layer], taps[moved(every, -a * spacing), :], TN) * grad_scale
            for b in range(3):
                conv_grad[layer, 3 * (a + 1) + b] = part_grad[:, b * channels : (b + 1) * channels]
        store(conv_grad.at[layer], conv_grad_hbm.at[layer], grad_sem.at[0, layer])
        store(proj_grad_ref.at[layer], proj_grad_hbm.at[layer], grad_sem.at[1, layer])
        gain_total = jnp.zeros((1, channels), jnp.float32)
        for part in chunks:
            rows = flat(part)
            normalized = normed[layer, rows, :]
            d_scaled = gather_rows(part, -spacing) * slope[layer, rows, :]
            gain_total = gain_total + jnp.sum(d_scaled * normalized, axis=0, keepdims=True)
            d_norm = d_scaled * gain
            delta = inv[layer, rows, :] * (
                d_norm - lane_mean(d_norm) - normalized * lane_mean(d_norm * normalized)
            )
            put(back, part, get(back, part) + delta)
        gain_grad_ref[layer : layer + 1, :] = gain_total * grad_scale

    final = back[:height, :height, :]
    rest = jnp.zeros((residues - height, channels), jnp.float32)
    d_row = jnp.concatenate([jnp.sum(final, axis=1), rest], axis=0).astype(jnp.bfloat16)
    d_col = jnp.concatenate([jnp.sum(final, axis=0), rest], axis=0).astype(jnp.bfloat16)
    embed_grad_ref[0] = dot(seq, d_row, TN) * grad_scale
    embed_grad_ref[1] = dot(seq, d_col, TN) * grad_scale
    store(gain_grad_ref, gain_grad_hbm, sem.at[1])
    store(embed_grad_ref, embed_grad_hbm, sem.at[2])
    seq_grad = (dot(d_row, embed[0], NT) + dot(d_col, embed[1], NT)) / math.sqrt(residues)
    first = own * (row * grid_cols + col)
    for k in range(own):
        chosen = lax.broadcasted_iota(jnp.int32, seq_grad.shape, 0) == first + k
        seq_grad_ref[k : k + 1, :] = jnp.sum(
            jnp.where(chosen, seq_grad, 0.0), axis=0, keepdims=True
        )
    store(seq_grad_ref, seq_grad_hbm, sem.at[3])
    for copy in stores:
        copy.wait()


def replicated_body(
    seq_feat, lengths, embed_weight, norm_gain, conv_weight, proj_weight, pair_cotangent
):
    tile_rows, tile_cols, channels = pair_cotangent.shape
    grid_rows, grid_cols = lax.axis_size("row"), lax.axis_size("col")
    residues = tile_rows * grid_rows
    height = most_live(residues)
    margin = 2 ** (LAYERS - 1)
    own, features = seq_feat.shape
    f32, bf16 = jnp.float32, jnp.bfloat16
    vmem = pl.BlockSpec(memory_space=pltpu.VMEM)
    hbm = pl.BlockSpec(memory_space=pltpu.HBM)
    square = (residues, residues, channels)
    payload = pl.pallas_call(
        pack_kernel,
        out_shape=pltpu.VMEM((tile_rows * tile_cols + 8, channels), bf16),
    )(in_hbm(seq_feat), in_hbm(pair_cotangent))
    payload = lax.optimization_barrier(payload)
    def swap(x, axis, count, bit):
        return lax.ppermute(x, axis, [(i, i ^ bit) for i in range(count)])

    ring = ring_order(grid_rows)
    turns = [
        lax.ppermute(
            payload,
            "row",
            [(ring[i], ring[(i + k) % grid_rows]) for i in range(grid_rows)],
        )
        for k in turn_order(grid_rows)
    ]
    column = lax.optimization_barrier(jnp.concatenate([payload] + turns, axis=0))
    column, lengths = lax.optimization_barrier((column, lengths))
    held = (
        embed_weight,
        norm_gain,
        conv_weight.reshape(LAYERS, 9 * channels, channels),
        proj_weight,
    )
    live, *held = pl.pallas_call(
        setup_kernel,
        out_shape=[pltpu.VMEM(square, f32)]
        + [pltpu.VMEM(x.shape, x.dtype) for x in held + (proj_weight,)],
        in_specs=[hbm] * (1 + len(held)),
        scratch_shapes=[
            pltpu.SMEM(lengths.shape, jnp.int32),
            pltpu.SemaphoreType.DMA((1 + len(held),)),
        ],
        cost_estimate=pl.CostEstimate(flops=0, bytes_accessed=4 * 2**20, transcendentals=0),
    )(in_hbm(lengths), *[in_hbm(x) for x in held])

    pieces = [column] + [swap(column, "col", grid_cols, k) for k in (3, 1, 2)]
    count = height * height
    edge = margin * height
    saved = (LAYERS, count, channels)
    results = (
        jax.ShapeDtypeStruct((tile_rows, tile_cols, channels), bf16),
        jax.ShapeDtypeStruct((own, features), f32),
        jax.ShapeDtypeStruct((2, features, channels), f32),
        jax.ShapeDtypeStruct((LAYERS, channels), f32),
        jax.ShapeDtypeStruct((LAYERS, 9, channels, channels), f32),
        jax.ShapeDtypeStruct((LAYERS, channels, channels), f32),
    )
    outs = pl.pallas_call(
        functools.partial(block_kernel, grid_rows, grid_cols),
        out_shape=results,
        in_specs=[vmem] * 10,
        out_specs=(hbm,) * len(results),
        scratch_shapes=[
            pltpu.VMEM(square, f32),
            pltpu.VMEM((count, channels), f32),
            pltpu.VMEM(square, f32),
            pltpu.VMEM((height, height + 2 * margin, channels), f32),
            pltpu.VMEM((count + 2 * edge, 3 * channels), bf16),
            pltpu.VMEM((count + 2 * edge, 3 * channels), f32),
            pltpu.VMEM(saved, f32),
            pltpu.VMEM(saved, f32),
            pltpu.VMEM(saved, f32),
            pltpu.VMEM(saved, bf16),
            pltpu.VMEM(saved, f32),
            pltpu.VMEM(saved, bf16),
            pltpu.VMEM((count, channels), bf16),
            pltpu.VMEM((8 * grid_rows * grid_cols, channels), f32),
            pltpu.VMEM((residues, channels), f32),
            pltpu.VMEM((residues, channels), f32),
            *[pltpu.VMEM(x.shape, x.dtype) for x in results],
            pltpu.SemaphoreType.DMA((4,)),
            pltpu.SemaphoreType.DMA((2, LAYERS)),
        ],
        compiler_params=pltpu.CompilerParams(vmem_limit_bytes=40 * 1024 * 1024),
    )(*pieces, live, *held)
    pair_output, seq_grad, embed_grad, gain_grad, conv_grad, proj_grad = outs
    return (
        pair_output,
        seq_grad,
        embed_grad,
        gain_grad,
        conv_grad.reshape(LAYERS, 3, 3, channels, channels),
        proj_grad,
    )


def map_fits(grid_cols, tile_rows, residues, channels):
    height = most_live(residues)
    held = height * height * channels * LAYERS * 24
    return grid_cols == 4 and tile_rows % 8 == 0 and height % CHUNK == 0 and held <= 16 * 2**20


def body(seq_feat, lengths, embed_weight, norm_gain, conv_weight, proj_weight, pair_cotangent):
    tile_rows, _, channels = pair_cotangent.shape
    residues = tile_rows * lax.axis_size("row")
    whole = map_fits(lax.axis_size("col"), tile_rows, residues, channels)
    plan = replicated_body if whole else tiled_body
    return plan(
        seq_feat, lengths, embed_weight, norm_gain, conv_weight, proj_weight, pair_cotangent
    )


def solution(mesh):
    placed = (
        P(("groups", "row", "col"), None),
        P("groups"),
        P(),
        P(),
        P(),
        P(),
        P(("groups", "row"), "col", None),
    )
    return jax.shard_map(
        body,
        mesh=mesh,
        in_specs=placed,
        out_specs=(
            P(("groups", "row"), "col", None),
            P(("groups", "row", "col"), None),
            P("groups", None, None),
            P("groups", None),
            P("groups", None, None, None, None),
            P("groups", None, None),
        ),
        check_vma=False,
    )
```
